128 devices in a mesh: wafer: 4 (over z), det: 32 (over y, x, core).
Axes of the slice: x: 4, y: 4, z: 4, core: 2. Of those that a mesh axis runs over, the one named last changes fastest.
Arguments:
- tod: float32 [8192, 8192], P(('wafer', 'det')), may hold values from -12 to 12
- gap_mask: int32 [8192, 8192], P(('wafer', 'det')), may hold values from 0 to 1
- coupling: float32 [8192, 32], P(('wafer', 'det')), may hold values from -5 to 5
- taps: float32 [129], replicated, may hold values from -1 to 1
- cross_det: int32 [8192], P(('wafer', 'det')), may hold values from 0 to 63
- cross_start: int32 [8192], P(('wafer', 'det')), may hold values from 0 to 7936
- cross_src: int32 [8192], P(('wafer', 'det')), may hold values from 0 to 127, as said below
- src_owner: int32 [128], replicated, may hold values from 0 to 127, as said below
Outputs:
- filled: float32 [8192, 8192], P(('wafer', 'det'))
- templates: float32 [4, 128, 256], P('wafer', 'det')
The draws below stay inside these ranges and needn't reach their ends.
Inputs may be any that keep to these rules, and one draw needn't show every extreme that they name: src_owner is a permutation of the template slots. `cross_src`: among one device's 64 crossings, at most 4 have slots in one block of 4 slots (o // 4 equal); in every device some block gets exactly 4.
All inputs are finite; a program needn't handle non-finite values.
Results may differ from the reference program's by a relative error of at most 0.00014.
Values sent between devices are 32-bit elements; how exact they have to be, the bound alone decides.
A program may use at most 64 MiB of HBM per device.

```python
import math
import jax
import jax.numpy as jnp
from jax import lax

D_DEV = 64
NS = 8192
M = 32
TAPS = 129
SNIP = 256
CROSS = 64
SRC_DEV = 4
DETS = 8192
NSRC = 128
CROSS_ALL = 8192
CAP = 4
WAFERS = 4


def crossing_tables(key):
    n_det = NSRC // SRC_DEV
    slots = n_det * CAP
    blocks = CROSS_ALL // CROSS
    key_owner, key_rows = jax.random.split(jax.random.fold_in(key, 7), 2)
    owner = jax.random.permutation(key_owner, NSRC).astype(jnp.int32)
    inverse = jnp.zeros((NSRC,), jnp.int32).at[owner].set(jnp.arange(NSRC, dtype=jnp.int32))

    def one_block(block_key):
        key_a, key_b, key_c, key_d = jax.random.split(block_key, 4)
        first = jax.random.randint(key_a, (), 0, n_det)
        priority = jax.random.permutation(key_b, slots).astype(jnp.int32)
        slot_ids = jnp.arange(slots, dtype=jnp.int32)
        priority = jnp.where(slot_ids // CAP == first, priority - slots, priority)
        chosen = jnp.argsort(priority, stable=True)[:CROSS].astype(jnp.int32)
        chosen = jax.random.permutation(key_c, chosen)
        target = chosen // CAP
        local = jax.random.randint(key_d, (CROSS,), 0, SRC_DEV)
        return inverse[(target * SRC_DEV + local).astype(jnp.int32)]
    sources = jax.vmap(one_block)(jax.random.split(key_rows, blocks)).reshape(-1)
    return (owner, sources.astype(jnp.int32))


def draw_src_owner(key, part):
    return crossing_tables(key)[0]


def draw_cross_src(key, part):
    return crossing_tables(key)[1]


def mode_tables(key):
    base = jax.random.fold_in(key, 11)
    key_c = jax.random.fold_in(base, 0)
    key_a = jax.random.fold_in(base, 2)
    key_f = jax.random.fold_in(base, 3)
    key_p = jax.random.fold_in(base, 4)
    key_r = jax.random.fold_in(base, 5)
    coupling = jnp.clip(jax.random.normal(key_c, (DETS, M), jnp.float32), -5.0, 5.0)
    strength = jnp.exp(jax.random.uniform(key_a, (M, 1), jnp.float32, math.log(0.1), math.log(0.5)))
    cycles = jax.random.randint(key_f, (M, 2), 1, 25).astype(jnp.int32)
    phase = jax.random.uniform(key_p, (M, 2), jnp.float32, -math.pi, math.pi)
    sample = jnp.arange(NS, dtype=jnp.int32)[None, :]
    first = (cycles[:, 0:1] * sample % NS).astype(jnp.float32) * (2.0 * math.pi / NS)
    second = (cycles[:, 1:2] * sample % NS).astype(jnp.float32) * (2.0 * math.pi / NS)
    slow = jnp.sin(first + phase[:, 0:1]) + 0.5 * jnp.sin(second + phase[:, 1:2])
    rough = 0.1 * jax.random.normal(key_r, (M, NS), jnp.float32)
    modes = strength * slow + rough
    return (coupling, modes)


def draw_coupling(key, part):
    return mode_tables(key)[0]


def draw_tod(key, part):
    coupling, modes = mode_tables(key)
    key_noise = jax.random.fold_in(key, 13)
    signal = jnp.clip(jax.random.normal(key_noise, (DETS, NS), jnp.float32), -4.0, 4.0)
    for mode in range(M):
        signal = signal + coupling[:, mode:mode + 1] * modes[mode:mode + 1, :]
    return jnp.clip(signal, -12.0, 12.0)


def draw_gap_mask(key, part):
    key_b, key_d, key_s, key_l, key_h, key_x = jax.random.split(jax.random.fold_in(key, 17), 6)
    events = 8
    blocks = DETS // D_DEV
    rows = jnp.arange(DETS, dtype=jnp.int32)
    block_of = (rows // D_DEV).astype(jnp.int32)
    times = jnp.arange(NS, dtype=jnp.int32)
    good = jax.random.randint(key_b, (DETS, NS), 0, 16) != 0
    alive = jax.random.randint(key_d, (DETS,), 0, 32) != 0
    starts = jax.random.randint(key_s, (events,), 0, NS)
    spans = jax.random.randint(key_l, (events,), NS // 64, NS // 8 + 1)
    share = jax.random.randint(key_h, (events,), 4, 13)
    votes = jax.random.randint(key_x, (events, blocks), 0, 16)
    struck_blocks = votes < share[:, None]
    for event in range(events):
        inside = (times - starts[event]) % NS < spans[event]
        struck = struck_blocks[event][block_of]
        good = good & jnp.logical_not(struck[:, None] & inside[None, :])
    good = good & alive[:, None]
    return good.astype(jnp.int32)


def place_ends(values, own_key, low, top_value):
    longest = values.shape.index(max(values.shape))
    spots = []
    for shift in (0, 1):
        where = [jax.random.randint(jax.random.fold_in(own_key, axis), (), 0, length) for axis, length in enumerate(values.shape)]
        where[longest] = (where[longest] + shift) % values.shape[longest]
        spots.append(tuple(where))
    return values.at[spots[0]].set(low).at[spots[1]].set(top_value)


def normal_values(stream_key, shape, deviation, most, held_as=jnp.bfloat16):
    return jnp.clip(deviation * jax.random.normal(stream_key, shape, jnp.float32), -most, most).astype(held_as)


def setup_inputs(seed: int = 0) -> dict:
    streams_of = jax.random.split(jax.random.key(seed), 9)
    tod = draw_tod(jax.random.fold_in(streams_of[8], 71), 0)
    gap_mask = draw_gap_mask(jax.random.fold_in(streams_of[8], 71), 0)
    coupling = draw_coupling(jax.random.fold_in(streams_of[8], 71), 0)
    taps = normal_values(streams_of[3], (TAPS,), (TAPS // 4) ** -0.5, 1.0, jnp.float32)
    cross_det = place_ends(jax.random.randint(streams_of[4], (CROSS_ALL,), 0, D_DEV), jax.random.fold_in(streams_of[4], 1), 0, D_DEV - 1).astype(jnp.int32)
    cross_start = place_ends(jax.random.randint(streams_of[5], (CROSS_ALL,), 0, NS - SNIP + 1), jax.random.fold_in(streams_of[5], 1), 0, NS - SNIP).astype(jnp.int32)
    cross_src = draw_cross_src(jax.random.fold_in(streams_of[8], 71), 0)
    src_owner = draw_src_owner(jax.random.fold_in(streams_of[8], 71), 0)
    return {"tod": tod, "gap_mask": gap_mask, "coupling": coupling, "taps": taps, "cross_det": cross_det, "cross_start": cross_start, "cross_src": cross_src, "src_owner": src_owner}


def correlate(resid, taps):
    half = (TAPS - 1) // 2
    out = lax.conv_general_dilated(resid[:, None, :], taps[None, None, :], (1,), [(half, half)], precision=lax.Precision.HIGHEST)
    return out[:, 0, :]


def reference(tod, gap_mask, coupling, taps, cross_det, cross_start, cross_src, src_owner):
    hi = lax.Precision.HIGHEST
    good = gap_mask.astype(jnp.float32)
    mode_sum = jnp.dot(coupling.T, good * tod, precision=hi)
    mode_weight = jnp.dot((coupling * coupling).T, good, precision=hi)
    amplitude = mode_sum / (mode_weight + 1.0)
    model = jnp.dot(coupling, amplitude, precision=hi)
    resid = good * (tod - model)
    smooth = correlate(resid, taps)
    filled = good * tod + (1.0 - good) * (model + smooth)
    rows = jnp.arange(CROSS_ALL, dtype=jnp.int32)
    device = rows // CROSS
    detector = (device * D_DEV + cross_det).astype(jnp.int32)

    def take(d, s):
        return lax.dynamic_slice(resid, (d, s), (1, SNIP))[0]

    snippet = jax.vmap(take)(detector, cross_start.astype(jnp.int32))
    group = device // (CROSS_ALL // CROSS // WAFERS)
    slot = src_owner[cross_src]
    seg = (group * NSRC + slot).astype(jnp.int32)
    sums = jax.ops.segment_sum(snippet, seg, num_segments=WAFERS * NSRC)
    counts = jax.ops.segment_sum(jnp.ones((CROSS_ALL,), jnp.float32), seg, num_segments=WAFERS * NSRC)
    templates = (sums / (counts + 1.0)[:, None]).reshape(WAFERS, NSRC, SNIP)
    return filled, templates
```

```python
import functools

import jax
import jax.numpy as jnp
from jax import lax
from jax.experimental import pallas as pl
from jax.experimental.pallas import tpu as pltpu
from jax.sharding import PartitionSpec as P

MESH = pl.DeviceIdType.MESH
F32 = jnp.float32
BF16 = jnp.bfloat16

ROWS = 64
NS = 8192
HALF = NS // 2
MODES = 32
TAPS = 129
CROSS = 64
RING = 4
DET = 32
SETS = (
    (0, 384, ("x", "y", "z")),
    (1536, 384, ("y", "z", "x")),
    (3072, 256, ("z", "x", "y")),
)
PLACE = (0, 384, 768)
BLOCKS = 1024


def split(v):
    hi = v.astype(BF16)
    lo = (v - hi.astype(F32)).astype(BF16)
    return hi, lo


def dot(a, b):
    return jnp.dot(a, b, preferred_element_type=F32)


def kernel(
    tod_hbm, mask_hbm, coup_ref, taps_ref, cdet_ref, cstart_ref, csrc_ref, owner_ref,
    filled_ref, templ_ref,
    tod, mask, model, res_hi, res_lo,
    part, acc, got_c, got1, acc1, got2, acc2, got3, amp,
    lhs_p, lhs_m, band,
    slots, dets, first_tile, shift, snip, cnt, cnt_got, tsum, tsum_got,
    in_sem, c_sem, r_sem, g_sem, gc_sem, t_sem,
):
    wafer = lax.axis_index("wafer")
    det = lax.axis_index("det")
    core = lax.rem(det, 2)
    x = lax.rem(lax.div(det, 2), RING)
    y = lax.div(det, 2 * RING)
    coord = {"x": x, "y": y, "z": wafer}

    def along(axis, step):
        xx, yy, zz = x, y, wafer
        if axis == "x":
            xx = lax.rem(x + step, RING)
        elif axis == "y":
            yy = lax.rem(y + step, RING)
        else:
            zz = lax.rem(wafer + step, RING)
        return (zz, (yy * RING + xx) * 2 + core)

    partner = (wafer, det + 1 - 2 * core)

    def remote(src, dst, send, recv, to):
        return pltpu.make_async_remote_copy(
            src_ref=src, dst_ref=dst, send_sem=send, recv_sem=recv,
            device_id=to, device_id_type=MESH,
        )

    def cols(first, width):
        return pl.ds(pl.multiple_of(first, 128), width)

    halves = (1 - core, core)
    loads = []
    for h in range(2):
        for s, (base, width, _) in enumerate(SETS):
            span = cols(halves[h] * HALF + base, RING * width)
            pair = (
                pltpu.make_async_copy(tod_hbm.at[:, span], tod.at[:, span], in_sem.at[h, s, 0]),
                pltpu.make_async_copy(mask_hbm.at[:, span], mask.at[:, span], in_sem.at[h, s, 1]),
            )
            for one in pair:
                one.start()
            loads.append(pair)

    barrier = pltpu.get_barrier_semaphore()
    for step in range(1, DET):
        pl.semaphore_signal(
            barrier, inc=1, device_id=(wafer, lax.rem(det + step, DET)), device_id_type=MESH
        )
    for step in range(1, RING):
        pl.semaphore_signal(barrier, inc=1, device_id=along("z", step), device_id_type=MESH)

    coup_t = coup_ref[...]
    c_hi, c_lo = split(coup_t.T)
    lhs_m[...] = jnp.concatenate([c_hi, c_lo, c_hi], axis=1)
    t_hi, t_lo = split(coup_t)
    w_hi, w_lo = split(coup_t * coup_t)
    zero = jnp.zeros((MODES, ROWS), BF16)
    lhs_p[0:32, :] = jnp.concatenate([t_hi, t_lo, t_hi, zero], axis=1)
    lhs_p[32:64, :] = jnp.concatenate([zero, zero, zero, w_hi], axis=1)
    lhs_p[64:96, :] = jnp.concatenate([zero, zero, zero, w_lo], axis=1)

    def partial_sums(first, width):
        span = cols(first, width)
        m = mask[:, span]
        v = jnp.where(m != 0, tod[:, span], 0.0)
        v_hi, v_lo = split(v)
        g = m.astype(F32).astype(BF16)
        out = dot(lhs_p[...], jnp.concatenate([v_hi, v_hi, v_lo, g], axis=0))
        return out[0:32], out[32:64] + out[64:96]

    def fill(h, s, dst):
        base, width, _ = SETS[s]
        for one in loads[h * 3 + s]:
            one.wait()

        def body(i, carry):
            local = base + i * width
            sums, weights = partial_sums(halves[h] * HALF + local, width)
            span = cols(local, width)
            for j in range(RING):
                dst[j, 0:8, span] = sums[8 * j:8 * j + 8]
                dst[j, 8:16, span] = weights[8 * j:8 * j + 8]
            return carry

        lax.fori_loop(0, RING, body, 0)

    copies_c = []
    for s, (base, width, _) in enumerate(SETS):
        span = pl.ds(base, RING * width)
        copies_c.append(
            remote(part.at[:, :, span], got_c.at[:, :, span], c_sem.at[s, 0], c_sem.at[s, 1], partner)
        )
    fill(0, 0, part)
    pl.semaphore_wait(barrier, DET - 1 + RING - 1)
    copies_c[0].start()
    for s in (1, 2):
        fill(0, s, part)
        copies_c[s].start()
    for s in range(3):
        fill(1, s, acc)

    owner = 2 * owner_ref[...]
    src_iota = lax.broadcasted_iota(jnp.int32, (128, CROSS), 0)
    of_src = (src_iota == csrc_ref[...]).astype(F32).astype(BF16)
    row_iota = lax.broadcasted_iota(jnp.int32, (256, 128), 0)
    perm0 = (row_iota == owner).astype(F32).astype(BF16)
    perm1 = (row_iota == owner + 1).astype(F32).astype(BF16)
    oh_t = jnp.concatenate([dot(perm0, of_src), dot(perm1, of_src)], axis=1)
    slots[:, 0:128] = oh_t.astype(BF16)
    slots[:, 128:256] = oh_t.astype(BF16)
    det_iota = lax.broadcasted_iota(jnp.int32, (ROWS, CROSS), 0)
    of_det = (det_iota == cdet_ref[...]).astype(F32).T.astype(BF16)
    dets[...] = jnp.concatenate([of_det, of_det], axis=1)
    start = jnp.broadcast_to(cstart_ref[...], (128, CROSS)).T
    first_tile[...] = start >> 7
    shift[...] = start & 127
    cnt[...] = jnp.broadcast_to(jnp.sum(oh_t, axis=1, keepdims=True), (256, 128)).reshape(DET, 8, 128)
    copies_n = []
    for step in range(1, DET):
        to = lax.rem(det + step, DET)
        copies_n.append(
            remote(cnt.at[to], cnt_got.at[step - 1], t_sem.at[0], t_sem.at[1], (wafer, to))
        )
        copies_n[-1].start()

    def exchange(sem, axis, src_of, dst_of):
        made = []
        for step in range(1, RING):
            made.append(
                remote(src_of(step), dst_of(step), sem.at[step - 1, 0], sem.at[step - 1, 1], along(axis, step))
            )
        for one in made:
            one.start()
        return made

    stage1 = []
    for s, (base, width, order) in enumerate(SETS):
        copies_c[s].wait_recv()
        span = pl.ds(base, RING * width)
        acc[:, :, span] += got_c[:, :, span]
        axis = order[0]

        def src_of(step, base=base, width=width, axis=axis):
            to = lax.rem(coord[axis] + step, RING)
            return acc.at[:, :, cols(base + to * width, width)]

        def dst_of(step, s=s, width=width):
            return got1.at[step - 1, :, :, pl.ds(PLACE[s], width)]

        stage1.append(exchange(r_sem.at[s, 0], axis, src_of, dst_of))

    row = lax.broadcasted_iota(jnp.int32, (256, 128), 0)
    col = lax.broadcasted_iota(jnp.int32, (256, 128), 1)
    pos = jnp.where(row < 192, row, row - 256)
    tap_of = pos - col + 64

    def add_tap(k, total):
        return total + jnp.where(tap_of == k, taps_ref[k], 0.0)

    b_hi, b_lo = split(lax.fori_loop(0, TAPS, add_tap, jnp.zeros((256, 128), F32)))
    band[:, 0:128] = b_hi
    band[:, 128:256] = b_lo

    stage2 = []
    for s, (base, width, order) in enumerate(SETS):
        for one in stage1[s]:
            one.wait_recv()
        mine = cols(base + coord[order[0]] * width, width)
        span = pl.ds(PLACE[s], width)
        acc1[:, :, span] = (acc[:, :, mine] + got1[0, :, :, span]) + (got1[1, :, :, span] + got1[2, :, :, span])
        axis = order[1]

        def src_of(step, span=span, axis=axis):
            return acc1.at[lax.rem(coord[axis] + step, RING), :, span]

        def dst_of(step, span=span):
            return got2.at[step - 1, :, span]

        stage2.append(exchange(r_sem.at[s, 1], axis, src_of, dst_of))

    stage3 = []
    for s, (base, width, order) in enumerate(SETS):
        for one in stage2[s]:
            one.wait_recv()
        span = pl.ds(PLACE[s], width)
        acc2[:, span] = (acc1[coord[order[1]], :, span] + got2[0, :, span]) + (got2[1, :, span] + got2[2, :, span])

        def src_of(step, span=span):
            return acc2.at[:, span]

        def dst_of(step, span=span):
            return got3.at[step - 1, :, span]

        stage3.append(exchange(r_sem.at[s, 2], order[2], src_of, dst_of))

    gather2 = []
    for s, (base, width, order) in enumerate(SETS):
        for one in stage3[s]:
            one.wait_recv()
        span = pl.ds(PLACE[s], width)
        whole = (acc2[:, span] + got3[0, :, span]) + (got3[1, :, span] + got3[2, :, span])
        block = cols(core * HALF + base + coord[order[0]] * width, width)
        amp[coord[order[1]], :, block] = whole[0:8] / (whole[8:16] + 1.0)

        def here(step, block=block, j=coord[order[1]]):
            return amp.at[j, :, block]

        gather2.append(exchange(g_sem.at[s, 0], order[1], here, here))

    gather1 = []
    for s, (base, width, order) in enumerate(SETS):
        for one in gather2[s]:
            one.wait_recv()
        block = cols(core * HALF + base + coord[order[0]] * width, width)

        def here(step, block=block):
            return amp.at[:, :, block]

        gather1.append(exchange(g_sem.at[s, 1], order[0], here, here))

    copies_a = []
    for s, (base, width, order) in enumerate(SETS):
        for one in gather1[s]:
            one.wait_recv()
        span = cols(core * HALF + base, RING * width)
        copies_a.append(remote(amp.at[:, :, span], amp.at[:, :, span], gc_sem.at[s, 0], gc_sem.at[s, 1], partner))
        copies_a[-1].start()
    for one in copies_a:
        one.wait_recv()

    for edge in (res_hi, res_lo):
        edge[:, 0:128] = jnp.zeros((ROWS, 128), BF16)
        edge[:, 128 + NS:256 + NS] = jnp.zeros((ROWS, 128), BF16)

    def model_block(b, wide):
        span = cols(b * 512, 512)
        a_hi, a_lo = split(amp[:, :, span].reshape(MODES, 512))
        value = dot(lhs_m[...], jnp.concatenate([a_hi, a_hi, a_lo], axis=0))
        model[:, span] = value
        r_hi, r_lo = split(jnp.where(mask[:, span] != 0, tod[:, span] - value, 0.0))
        res_hi[:, cols(b * 512 + 128, 512)] = r_hi
        res_lo[:, cols(b * 512 + 128, 512)] = r_lo
        lines = dot(dets[...], jnp.concatenate([r_hi, r_lo], axis=0))
        tile = first_tile[...]
        wide = list(wide)
        for q in range(4):
            for w in range(3):
                wide[w] = jnp.where(tile == b * 4 + q - w, lines[:, 128 * q:128 * q + 128], wide[w])
        return tuple(wide)

    wide = lax.fori_loop(0, NS // 512, model_block, (jnp.zeros((CROSS, 128), F32),) * 3)

    rows = jnp.concatenate(wide, axis=1)
    rest = jnp.concatenate([shift[...]] * 3, axis=1)
    for bit in range(7):
        moved = pltpu.roll(rows, 384 - (1 << bit), 1)
        rows = jnp.where((rest & (1 << bit)) != 0, moved, rows)
    snip[0:CROSS, :] = rows[:, 0:128]
    snip[CROSS:2 * CROSS, :] = rows[:, 128:256]
    s_hi, s_lo = split(snip[...])
    tsum[...] = dot(slots[...], jnp.concatenate([s_hi, s_lo], axis=0)).reshape(DET, 8, 128)
    copies_t = []
    for step in range(1, DET):
        to = lax.rem(det + step, DET)
        copies_t.append(
            remote(tsum.at[to], tsum_got.at[step - 1], t_sem.at[2], t_sem.at[3], (wafer, to))
        )
        copies_t[-1].start()

    lane64 = lax.broadcasted_iota(jnp.int32, (ROWS, 128), 1) < 64

    def fill_block(b, carry):
        pieces = []
        for res in (res_hi, res_lo):
            left = []
            for q in range(4):
                before = res[:, cols(b * 512 + q * 128, 128)]
                here = res[:, cols(b * 512 + q * 128 + 128, 128)]
                after = res[:, cols(b * 512 + q * 128 + 256, 128)]
                left.append(jnp.concatenate([here, jnp.where(lane64, after, before)], axis=1))
            pieces.append(jnp.concatenate(left, axis=0))
        l_hi, l_lo = pieces
        first = dot(l_hi, band[...])
        second = dot(l_lo, band[:, 0:128])
        smooth = first[:, 0:128] + (first[:, 128:256] + second)
        for q in range(4):
            span = cols(b * 512 + q * 128, 128)
            filled_ref[:, span] = jnp.where(
                mask[:, span] != 0, tod[:, span], model[:, span] + smooth[q * ROWS:(q + 1) * ROWS]
            )
        return carry

    lax.fori_loop(0, NS // 512, fill_block, 0)

    def wait_all(src, dst, send, recv):
        every = remote(src.at[0:DET - 1], dst.at[0:DET - 1], send, recv, partner)
        every.wait_recv()
        every.wait_send()

    wait_all(cnt, cnt_got, t_sem.at[0], t_sem.at[1])
    wait_all(tsum, tsum_got, t_sem.at[2], t_sem.at[3])
    number = cnt[det]
    total = tsum[det]
    for step in range(DET - 1):
        number += cnt_got[step]
        total += tsum_got[step]
    snip[0:8, :] = total / (number + 1.0)
    for o in range(4):
        templ_ref[0, o:o + 1, 0:128] = snip[2 * o:2 * o + 1, :]
        templ_ref[0, o:o + 1, 128:256] = snip[2 * o + 1:2 * o + 2, :]

    for one in copies_c + copies_a:
        one.wait_send()
    for group in stage1 + stage2 + stage3 + gather2 + gather1:
        for one in group:
            one.wait_send()


def on_device(tod, gap_mask, coupling, taps, cross_det, cross_start, cross_src, src_owner):
    vmem, smem, hbm = (pl.BlockSpec(memory_space=m) for m in (pltpu.VMEM, pltpu.SMEM, pltpu.HBM))
    return pl.pallas_call(
        kernel,
        out_shape=(
            jax.ShapeDtypeStruct((ROWS, NS), F32),
            jax.ShapeDtypeStruct((1, 4, 256), F32),
        ),
        in_specs=[hbm, hbm, vmem, smem, vmem, vmem, vmem, vmem],
        out_specs=(vmem, vmem),
        scratch_shapes=[
            pltpu.VMEM((ROWS, NS), F32),
            pltpu.VMEM((ROWS, NS), jnp.int32),
            pltpu.VMEM((ROWS, NS), F32),
            pltpu.VMEM((ROWS, NS + 256), BF16),
            pltpu.VMEM((ROWS, NS + 256), BF16),
            pltpu.VMEM((RING, 16, HALF), F32),
            pltpu.VMEM((RING, 16, HALF), F32),
            pltpu.VMEM((RING, 16, HALF), F32),
            pltpu.VMEM((3, RING, 16, BLOCKS), F32),
            pltpu.VMEM((RING, 16, BLOCKS), F32),
            pltpu.VMEM((3, 16, BLOCKS), F32),
            pltpu.VMEM((16, BLOCKS), F32),
            pltpu.VMEM((3, 16, BLOCKS), F32),
            pltpu.VMEM((RING, 8, NS), F32),
            pltpu.VMEM((96, 256), BF16),
            pltpu.VMEM((ROWS, 96), BF16),
            pltpu.VMEM((256, 256), BF16),
            pltpu.VMEM((256, 256), BF16),
            pltpu.VMEM((CROSS, 128), BF16),
            pltpu.VMEM((CROSS, 128), jnp.int32),
            pltpu.VMEM((CROSS, 128), jnp.int32),
            pltpu.VMEM((2 * CROSS, 128), F32),
            pltpu.VMEM((DET, 8, 128), F32),
            pltpu.VMEM((DET, 8, 128), F32),
            pltpu.VMEM((DET, 8, 128), F32),
            pltpu.VMEM((DET, 8, 128), F32),
            pltpu.SemaphoreType.DMA((2, 3, 2)),
            pltpu.SemaphoreType.DMA((3, 2)),
            pltpu.SemaphoreType.DMA((3, 3, 3, 2)),
            pltpu.SemaphoreType.DMA((3, 2, 3, 2)),
            pltpu.SemaphoreType.DMA((3, 2)),
            pltpu.SemaphoreType.DMA((4,)),
        ],
        compiler_params=pltpu.CompilerParams(
            collective_id=0, has_side_effects=True, vmem_limit_bytes=48 << 20
        ),
    )(tod, gap_mask, coupling.T, taps, *(v.reshape(1, -1) for v in (cross_det, cross_start, cross_src, src_owner)))


def solution(mesh):
    return jax.shard_map(
        on_device,
        mesh=mesh,
        in_specs=(
            P(("wafer", "det"), None),
            P(("wafer", "det"), None),
            P(("wafer", "det"), None),
            P(),
            P(("wafer", "det")),
            P(("wafer", "det")),
            P(("wafer", "det")),
            P(),
        ),
        out_specs=(P(("wafer", "det"), None), P("wafer", "det", None)),
        check_vma=False,
    )
```

```python
import functools

import jax
import jax.numpy as jnp
from jax import lax
from jax.experimental import pallas as pl
from jax.experimental.pallas import tpu as pltpu
from jax.sharding import PartitionSpec as P

MESH = pl.DeviceIdType.MESH
F32 = jnp.float32
BF16 = jnp.bfloat16

ROWS = 64
NS = 8192
HALF = NS // 2
MODES = 32
TAPS = 129
CROSS = 64
RING = 4
DET = 32
SETS = (
    (0, 384, ("x", "y", "z")),
    (1536, 384, ("y", "z", "x")),
    (3072, 256, ("z", "x", "y")),
)
PLACE = (0, 384, 768)
BLOCKS = 1024


def split(v):
    hi = v.astype(BF16)
    lo = (v - hi.astype(F32)).astype(BF16)
    return hi, lo


def dot(a, b):
    return jnp.dot(a, b, preferred_element_type=F32)


def kernel(
    tod_hbm, mask_hbm, coup_hbm, taps_hbm, cdet_hbm, cstart_hbm, csrc_hbm, owner_hbm,
    filled_hbm, templ_ref,
    coup_ref, taps_ref, cdet_ref, cstart_ref, csrc_ref, owner_ref, filled,
    tod, mask, model, res_hi, res_lo,
    part, acc, got_c, got1, acc1, got2, acc2, got3, amp,
    lhs_p, lhs_m, band,
    slots, dets, first_tile, shift, snip, cnt, cnt_got, tsum, tsum_got,
    in_sem, small_sem, out_sem, c_sem, r_sem, g_sem, gc_sem, t_sem,
):
    wafer = lax.axis_index("wafer")
    det = lax.axis_index("det")
    core = lax.rem(det, 2)
    x = lax.rem(lax.div(det, 2), RING)
    y = lax.div(det, 2 * RING)
    coord = {"x": x, "y": y, "z": wafer}

    def along(axis, step):
        xx, yy, zz = x, y, wafer
        if axis == "x":
            xx = lax.rem(x + step, RING)
        elif axis == "y":
            yy = lax.rem(y + step, RING)
        else:
            zz = lax.rem(wafer + step, RING)
        return (zz, (yy * RING + xx) * 2 + core)

    partner = (wafer, det + 1 - 2 * core)

    def remote(src, dst, send, recv, to):
        return pltpu.make_async_remote_copy(
            src_ref=src, dst_ref=dst, send_sem=send, recv_sem=recv,
            device_id=to, device_id_type=MESH,
        )

    def cols(first, width):
        return pl.ds(pl.multiple_of(first, 128), width)

    small = []
    for k, (src, dst) in enumerate((
        (coup_hbm, coup_ref), (taps_hbm, taps_ref), (cdet_hbm, cdet_ref),
        (cstart_hbm, cstart_ref), (csrc_hbm, csrc_ref), (owner_hbm, owner_ref),
    )):
        small.append(pltpu.make_async_copy(src, dst, small_sem.at[k]))
        small[-1].start()

    halves = (1 - core, core)
    loads = []
    for h in range(2):
        for s, (base, width, _) in enumerate(SETS):
            span = cols(halves[h] * HALF + base, RING * width)
            pair = (
                pltpu.make_async_copy(tod_hbm.at[:, span], tod.at[:, span], in_sem.at[h, s, 0]),
                pltpu.make_async_copy(mask_hbm.at[:, span], mask.at[:, span], in_sem.at[h, s, 1]),
            )
            for one in pair:
                one.start()
            loads.append(pair)

    barrier = pltpu.get_barrier_semaphore()
    for step in range(1, DET):
        pl.semaphore_signal(
            barrier, inc=1, device_id=(wafer, lax.rem(det + step, DET)), device_id_type=MESH
        )
    for step in range(1, RING):
        pl.semaphore_signal(barrier, inc=1, device_id=along("z", step), device_id_type=MESH)

    small[0].wait()
    coup_t = coup_ref[...]
    c_hi, c_lo = split(coup_t.T)
    lhs_m[...] = jnp.concatenate([c_hi, c_lo, c_hi], axis=1)
    t_hi, t_lo = split(coup_t)
    w_hi, w_lo = split(coup_t * coup_t)
    zero = jnp.zeros((MODES, ROWS), BF16)
    lhs_p[0:32, :] = jnp.concatenate([t_hi, t_lo, t_hi, zero], axis=1)
    lhs_p[32:64, :] = jnp.concatenate([zero, zero, zero, w_hi], axis=1)
    lhs_p[64:96, :] = jnp.concatenate([zero, zero, zero, w_lo], axis=1)

    def partial_sums(first, width):
        span = cols(first, width)
        m = mask[:, span]
        v = jnp.where(m != 0, tod[:, span], 0.0)
        v_hi, v_lo = split(v)
        g = m.astype(F32).astype(BF16)
        out = dot(lhs_p[...], jnp.concatenate([v_hi, v_hi, v_lo, g], axis=0))
        return out[0:32], out[32:64] + out[64:96]

    def fill(h, s, dst):
        base, width, _ = SETS[s]
        for one in loads[h * 3 + s]:
            one.wait()

        def body(i, carry):
            local = base + i * width
            sums, weights = partial_sums(halves[h] * HALF + local, width)
            span = cols(local, width)
            for j in range(RING):
                dst[j, 0:8, span] = sums[8 * j:8 * j + 8]
                dst[j, 8:16, span] = weights[8 * j:8 * j + 8]
            return carry

        lax.fori_loop(0, RING, body, 0)

    copies_c = []
    for s, (base, width, _) in enumerate(SETS):
        span = pl.ds(base, RING * width)
        copies_c.append(
            remote(part.at[:, :, span], got_c.at[:, :, span], c_sem.at[s, 0], c_sem.at[s, 1], partner)
        )
    fill(0, 0, part)
    pl.semaphore_wait(barrier, DET - 1 + RING - 1)
    copies_c[0].start()
    for s in (1, 2):
        fill(0, s, part)
        copies_c[s].start()
    for s in range(3):
        fill(1, s, acc)

    for one in small[2:]:
        one.wait()
    owner = 2 * owner_ref[...]
    src_iota = lax.broadcasted_iota(jnp.int32, (128, CROSS), 0)
    of_src = (src_iota == csrc_ref[...]).astype(F32).astype(BF16)
    row_iota = lax.broadcasted_iota(jnp.int32, (256, 128), 0)
    perm0 = (row_iota == owner).astype(F32).astype(BF16)
    perm1 = (row_iota == owner + 1).astype(F32).astype(BF16)
    oh_t = jnp.concatenate([dot(perm0, of_src), dot(perm1, of_src)], axis=1)
    slots[:, 0:128] = oh_t.astype(BF16)
    slots[:, 128:256] = oh_t.astype(BF16)
    det_iota = lax.broadcasted_iota(jnp.int32, (ROWS, CROSS), 0)
    of_det = (det_iota == cdet_ref[...]).astype(F32).T.astype(BF16)
    dets[...] = jnp.concatenate([of_det, of_det], axis=1)
    start = jnp.broadcast_to(cstart_ref[...], (128, CROSS)).T
    first_tile[...] = start >> 7
    shift[...] = start & 127
    cnt[...] = jnp.broadcast_to(jnp.sum(oh_t, axis=1, keepdims=True), (256, 128)).reshape(DET, 8, 128)
    copies_n = []
    for step in range(1, DET):
        to = lax.rem(det + step, DET)
        copies_n.append(
            remote(cnt.at[to], cnt_got.at[step - 1], t_sem.at[0], t_sem.at[1], (wafer, to))
        )
        copies_n[-1].start()

    def exchange(sem, axis, src_of, dst_of):
        made = []
        for step in range(1, RING):
            made.append(
                remote(src_of(step), dst_of(step), sem.at[step - 1, 0], sem.at[step - 1, 1], along(axis, step))
            )
        for one in made:
            one.start()
        return made

    stage1 = []
    for s, (base, width, order) in enumerate(SETS):
        copies_c[s].wait_recv()
        span = pl.ds(base, RING * width)
        acc[:, :, span] += got_c[:, :, span]
        axis = order[0]

        def src_of(step, base=base, width=width, axis=axis):
            to = lax.rem(coord[axis] + step, RING)
            return acc.at[:, :, cols(base + to * width, width)]

        def dst_of(step, s=s, width=width):
            return got1.at[step - 1, :, :, pl.ds(PLACE[s], width)]

        stage1.append(exchange(r_sem.at[s, 0], axis, src_of, dst_of))

    small[1].wait()
    line = jnp.concatenate([taps_ref[...], jnp.zeros((1, 256 - TAPS), F32)], axis=1)
    turned = pltpu.roll(jnp.broadcast_to(line, (128, 256)), 192, 1, stride=1, stride_axis=0)
    b_hi, b_lo = split(turned.T)
    band[:, 0:128] = b_hi
    band[:, 128:256] = b_lo

    stage2 = []
    for s, (base, width, order) in enumerate(SETS):
        for one in stage1[s]:
            one.wait_recv()
        mine = cols(base + coord[order[0]] * width, width)
        span = pl.ds(PLACE[s], width)
        acc1[:, :, span] = (acc[:, :, mine] + got1[0, :, :, span]) + (got1[1, :, :, span] + got1[2, :, :, span])
        axis = order[1]

        def src_of(step, span=span, axis=axis):
            return acc1.at[lax.rem(coord[axis] + step, RING), :, span]

        def dst_of(step, span=span):
            return got2.at[step - 1, :, span]

        stage2.append(exchange(r_sem.at[s, 1], axis, src_of, dst_of))

    stage3 = []
    for s, (base, width, order) in enumerate(SETS):
        for one in stage2[s]:
            one.wait_recv()
        span = pl.ds(PLACE[s], width)
        acc2[:, span] = (acc1[coord[order[1]], :, span] + got2[0, :, span]) + (got2[1, :, span] + got2[2, :, span])

        def src_of(step, span=span):
            return acc2.at[:, span]

        def dst_of(step, span=span):
            return got3.at[step - 1, :, span]

        stage3.append(exchange(r_sem.at[s, 2], order[2], src_of, dst_of))

    gather2 = []
    for s, (base, width, order) in enumerate(SETS):
        for one in stage3[s]:
            one.wait_recv()
        span = pl.ds(PLACE[s], width)
        whole = (acc2[:, span] + got3[0, :, span]) + (got3[1, :, span] + got3[2, :, span])
        block = cols(core * HALF + base + coord[order[0]] * width, width)
        amp[coord[order[1]], :, block] = whole[0:8] / (whole[8:16] + 1.0)

        def here(step, block=block, j=coord[order[1]]):
            return amp.at[j, :, block]

        gather2.append(exchange(g_sem.at[s, 0], order[1], here, here))

    gather1 = []
    for s, (base, width, order) in enumerate(SETS):
        for one in gather2[s]:
            one.wait_recv()
        block = cols(core * HALF + base + coord[order[0]] * width, width)

        def here(step, block=block):
            return amp.at[:, :, block]

        gather1.append(exchange(g_sem.at[s, 1], order[0], here, here))

    copies_a = []
    for s, (base, width, order) in enumerate(SETS):
        for one in gather1[s]:
            one.wait_recv()
        span = cols(core * HALF + base, RING * width)
        copies_a.append(remote(amp.at[:, :, span], amp.at[:, :, span], gc_sem.at[s, 0], gc_sem.at[s, 1], partner))
        copies_a[-1].start()
    for one in copies_a:
        one.wait_recv()

    for edge in (res_hi, res_lo):
        edge[:, 0:128] = jnp.zeros((ROWS, 128), BF16)
        edge[:, 128 + NS:256 + NS] = jnp.zeros((ROWS, 128), BF16)

    def model_block(b, wide):
        span = cols(b * 512, 512)
        a_hi, a_lo = split(amp[:, :, span].reshape(MODES, 512))
        value = dot(lhs_m[...], jnp.concatenate([a_hi, a_hi, a_lo], axis=0))
        model[:, span] = value
        r_hi, r_lo = split(jnp.where(mask[:, span] != 0, tod[:, span] - value, 0.0))
        res_hi[:, cols(b * 512 + 128, 512)] = r_hi
        res_lo[:, cols(b * 512 + 128, 512)] = r_lo
        lines = dot(dets[...], jnp.concatenate([r_hi, r_lo], axis=0))
        tile = first_tile[...]
        wide = list(wide)
        for q in range(4):
            for w in range(3):
                wide[w] = jnp.where(tile == b * 4 + q - w, lines[:, 128 * q:128 * q + 128], wide[w])
        return tuple(wide)

    wide = lax.fori_loop(0, NS // 512, model_block, (jnp.zeros((CROSS, 128), F32),) * 3)

    rows = jnp.concatenate(wide, axis=1)
    rest = jnp.concatenate([shift[...]] * 3, axis=1)
    for bit in range(7):
        moved = pltpu.roll(rows, 384 - (1 << bit), 1)
        rows = jnp.where((rest & (1 << bit)) != 0, moved, rows)
    snip[0:CROSS, :] = rows[:, 0:128]
    snip[CROSS:2 * CROSS, :] = rows[:, 128:256]
    s_hi, s_lo = split(snip[...])
    tsum[...] = dot(slots[...], jnp.concatenate([s_hi, s_lo], axis=0)).reshape(DET, 8, 128)
    copies_t = []
    for step in range(1, DET):
        to = lax.rem(det + step, DET)
        copies_t.append(
            remote(tsum.at[to], tsum_got.at[step - 1], t_sem.at[2], t_sem.at[3], (wafer, to))
        )
        copies_t[-1].start()

    lane64 = lax.broadcasted_iota(jnp.int32, (ROWS, 128), 1) < 64

    def fill_block(b, carry):
        pieces = []
        for res in (res_hi, res_lo):
            left = []
            for q in range(4):
                before = res[:, cols(b * 512 + q * 128, 128)]
                here = res[:, cols(b * 512 + q * 128 + 128, 128)]
                after = res[:, cols(b * 512 + q * 128 + 256, 128)]
                left.append(jnp.concatenate([here, jnp.where(lane64, after, before)], axis=1))
            pieces.append(jnp.concatenate(left, axis=0))
        l_hi, l_lo = pieces
        first = dot(l_hi, band[...])
        second = dot(l_lo, band[:, 0:128])
        smooth = first[:, 0:128] + (first[:, 128:256] + second)
        for q in range(4):
            span = cols(b * 512 + q * 128, 128)
            filled[:, span] = jnp.where(
                mask[:, span] != 0, tod[:, span], model[:, span] + smooth[q * ROWS:(q + 1) * ROWS]
            )
        return carry

    outs = []
    for part_of in range(4):
        lax.fori_loop(part_of * 4, part_of * 4 + 4, fill_block, 0)
        span = pl.ds(part_of * 2048, 2048)
        outs.append(pltpu.make_async_copy(filled.at[:, span], filled_hbm.at[:, span], out_sem.at[part_of]))
        outs[-1].start()

    def wait_all(src, dst, send, recv):
        every = remote(src.at[0:DET - 1], dst.at[0:DET - 1], send, recv, partner)
        every.wait_recv()
        every.wait_send()

    wait_all(cnt, cnt_got, t_sem.at[0], t_sem.at[1])
    wait_all(tsum, tsum_got, t_sem.at[2], t_sem.at[3])
    number = cnt[det]
    total = tsum[det]
    for step in range(DET - 1):
        number += cnt_got[step]
        total += tsum_got[step]
    snip[0:8, :] = total / (number + 1.0)
    for o in range(4):
        templ_ref[0, o:o + 1, 0:128] = snip[2 * o:2 * o + 1, :]
        templ_ref[0, o:o + 1, 128:256] = snip[2 * o + 1:2 * o + 2, :]

    for one in outs:
        one.wait()
    for one in copies_c + copies_a:
        one.wait_send()
    for group in stage1 + stage2 + stage3 + gather2 + gather1:
        for one in group:
            one.wait_send()


def on_device(tod, gap_mask, coupling, taps, cross_det, cross_start, cross_src, src_owner):
    vmem, hbm = (pl.BlockSpec(memory_space=m) for m in (pltpu.VMEM, pltpu.HBM))
    return pl.pallas_call(
        kernel,
        out_shape=(
            jax.ShapeDtypeStruct((ROWS, NS), F32),
            jax.ShapeDtypeStruct((1, 4, 256), F32),
        ),
        in_specs=[hbm] * 8,
        out_specs=(hbm, vmem),
        scratch_shapes=[
            pltpu.VMEM((MODES, ROWS), F32),
            pltpu.VMEM((1, TAPS), F32),
            pltpu.VMEM((1, CROSS), jnp.int32),
            pltpu.VMEM((1, CROSS), jnp.int32),
            pltpu.VMEM((1, CROSS), jnp.int32),
            pltpu.VMEM((1, 128), jnp.int32),
            pltpu.VMEM((ROWS, NS), F32),
            pltpu.VMEM((ROWS, NS), F32),
            pltpu.VMEM((ROWS, NS), jnp.int32),
            pltpu.VMEM((ROWS, NS), F32),
            pltpu.VMEM((ROWS, NS + 256), BF16),
            pltpu.VMEM((ROWS, NS + 256), BF16),
            pltpu.VMEM((RING, 16, HALF), F32),
            pltpu.VMEM((RING, 16, HALF), F32),
            pltpu.VMEM((RING, 16, HALF), F32),
            pltpu.VMEM((3, RING, 16, BLOCKS), F32),
            pltpu.VMEM((RING, 16, BLOCKS), F32),
            pltpu.VMEM((3, 16, BLOCKS), F32),
            pltpu.VMEM((16, BLOCKS), F32),
            pltpu.VMEM((3, 16, BLOCKS), F32),
            pltpu.VMEM((RING, 8, NS), F32),
            pltpu.VMEM((96, 256), BF16),
            pltpu.VMEM((ROWS, 96), BF16),
            pltpu.VMEM((256, 256), BF16),
            pltpu.VMEM((256, 256), BF16),
            pltpu.VMEM((CROSS, 128), BF16),
            pltpu.VMEM((CROSS, 128), jnp.int32),
            pltpu.VMEM((CROSS, 128), jnp.int32),
            pltpu.VMEM((2 * CROSS, 128), F32),
            pltpu.VMEM((DET, 8, 128), F32),
            pltpu.VMEM((DET, 8, 128), F32),
            pltpu.VMEM((DET, 8, 128), F32),
            pltpu.VMEM((DET, 8, 128), F32),
            pltpu.SemaphoreType.DMA((2, 3, 2)),
            pltpu.SemaphoreType.DMA((6,)),
            pltpu.SemaphoreType.DMA((4,)),
            pltpu.SemaphoreType.DMA((3, 2)),
            pltpu.SemaphoreType.DMA((3, 3, 3, 2)),
            pltpu.SemaphoreType.DMA((3, 2, 3, 2)),
            pltpu.SemaphoreType.DMA((3, 2)),
            pltpu.SemaphoreType.DMA((4,)),
        ],
        compiler_params=pltpu.CompilerParams(
            collective_id=0, has_side_effects=True, vmem_limit_bytes=67043328
        ),
    )(tod, gap_mask, coupling.T, *(v.reshape(1, -1) for v in (taps, cross_det, cross_start, cross_src, src_owner)))


def solution(mesh):
    return jax.shard_map(
        on_device,
        mesh=mesh,
        in_specs=(
            P(("wafer", "det"), None),
            P(("wafer", "det"), None),
            P(("wafer", "det"), None),
            P(),
            P(("wafer", "det")),
            P(("wafer", "det")),
            P(("wafer", "det")),
            P(),
        ),
        out_specs=(P(("wafer", "det"), None), P("wafer", "det", None)),
        check_vma=False,
    )
```

```python
import functools

import jax
import jax.numpy as jnp
from jax import lax
from jax.experimental import pallas as pl
from jax.experimental.pallas import tpu as pltpu
from jax.sharding import PartitionSpec as P

MESH = pl.DeviceIdType.MESH
F32 = jnp.float32
BF16 = jnp.bfloat16

ROWS = 64
NS = 8192
HALF = NS // 2
MODES = 32
TAPS = 129
CROSS = 64
RING = 4
DET = 32
SETS = (
    (0, 384, ("x", "y", "z")),
    (1536, 384, ("y", "z", "x")),
    (3072, 256, ("z", "x", "y")),
)
PLACE = (0, 384, 768)
BLOCKS = 1024


def split(v):
    hi = v.astype(BF16)
    lo = (v - hi.astype(F32)).astype(BF16)
    return hi, lo


def dot(a, b):
    return jnp.dot(a, b, preferred_element_type=F32)


def kernel(
    tod_hbm, mask_hbm, coup_hbm, taps_hbm, cdet_hbm, cstart_hbm, csrc_hbm, owner_hbm,
    filled_hbm, templ_ref,
    coup_ref, taps_ref, cdet_ref, cstart_ref, csrc_ref, owner_ref, filled,
    tod, mask, model, res_hi, res_lo,
    part, acc, got_c, got_p, acc2, got3, amp,
    lhs_p, lhs_m, band,
    slots, dets, first_tile, shift, snip, cnt, cnt_got, tsum, tsum_got,
    in_sem, small_sem, out_sem, ready_sem, c_sem, p_sem, r_sem, g_sem, gc_sem, t_sem,
):
    wafer = lax.axis_index("wafer")
    det = lax.axis_index("det")
    core = lax.rem(det, 2)
    x = lax.rem(lax.div(det, 2), RING)
    y = lax.div(det, 2 * RING)
    coord = {"x": x, "y": y, "z": wafer}

    def reach(steps):
        at = {a: lax.rem(coord[a] + steps[a], RING) if steps.get(a) else coord[a] for a in coord}
        return (at["z"], (at["y"] * RING + at["x"]) * 2 + core)

    partner = (wafer, det + 1 - 2 * core)

    def remote(src, dst, send, recv, to):
        return pltpu.make_async_remote_copy(
            src_ref=src, dst_ref=dst, send_sem=send, recv_sem=recv,
            device_id=to, device_id_type=MESH,
        )

    def cols(first, width):
        return pl.ds(pl.multiple_of(first, 128), width)

    small = []
    for k, (src, dst) in enumerate((
        (coup_hbm, coup_ref), (taps_hbm, taps_ref), (cdet_hbm, cdet_ref),
        (cstart_hbm, cstart_ref), (csrc_hbm, csrc_ref), (owner_hbm, owner_ref),
    )):
        small.append(pltpu.make_async_copy(src, dst, small_sem.at[k]))
        small[-1].start()

    halves = (1 - core, core)
    loads = []
    for h in range(2):
        for s, (base, width, _) in enumerate(SETS):
            span = cols(halves[h] * HALF + base, RING * width)
            pair = (
                pltpu.make_async_copy(tod_hbm.at[:, span], tod.at[:, span], in_sem.at[h, s, 0]),
                pltpu.make_async_copy(mask_hbm.at[:, span], mask.at[:, span], in_sem.at[h, s, 1]),
            )
            for one in pair:
                one.start()
            loads.append(pair)

    lines = [reach({a: step}) for a in ("x", "y", "z") for step in range(1, RING)]
    barrier = pltpu.get_barrier_semaphore()
    for to in [partner] + lines:
        pl.semaphore_signal(barrier, inc=1, device_id=to, device_id_type=MESH)

    small[0].wait()
    coup_t = coup_ref[...]
    c_hi, c_lo = split(coup_t.T)
    lhs_m[...] = jnp.concatenate([c_hi, c_lo, c_hi], axis=1)
    t_hi, t_lo = split(coup_t)
    w_hi, w_lo = split(coup_t * coup_t)
    zero = jnp.zeros((MODES, ROWS), BF16)
    lhs_p[0:32, :] = jnp.concatenate([t_hi, t_lo, t_hi, zero], axis=1)
    lhs_p[32:64, :] = jnp.concatenate([zero, zero, zero, w_hi], axis=1)
    lhs_p[64:96, :] = jnp.concatenate([zero, zero, zero, w_lo], axis=1)

    def partial_sums(first, width):
        span = cols(first, width)
        m = mask[:, span]
        v = jnp.where(m != 0, tod[:, span], 0.0)
        v_hi, v_lo = split(v)
        g = m.astype(F32).astype(BF16)
        out = dot(lhs_p[...], jnp.concatenate([v_hi, v_hi, v_lo, g], axis=0))
        return out[0:32], out[32:64] + out[64:96]

    def fill(h, s, dst):
        base, width, _ = SETS[s]
        for one in loads[h * 3 + s]:
            one.wait()

        def body(i, carry):
            local = base + i * width
            sums, weights = partial_sums(halves[h] * HALF + local, width)
            span = cols(local, width)
            for j in range(RING):
                dst[j, 0:8, span] = sums[8 * j:8 * j + 8]
                dst[j, 8:16, span] = weights[8 * j:8 * j + 8]
            return carry

        lax.fori_loop(0, RING, body, 0)

    copies_c = []
    for s, (base, width, _) in enumerate(SETS):
        span = pl.ds(base, RING * width)
        copies_c.append(
            remote(part.at[:, :, span], got_c.at[:, :, span], c_sem.at[s, 0], c_sem.at[s, 1], partner)
        )
    fill(0, 0, part)
    pl.semaphore_wait(barrier, 1 + len(lines))
    copies_c[0].start()
    for to in lines:
        pl.semaphore_signal(ready_sem, inc=1, device_id=to, device_id_type=MESH)
    for s in (1, 2):
        fill(0, s, part)
        copies_c[s].start()
    for s in range(3):
        fill(1, s, acc)

    for one in small[2:]:
        one.wait()
    owner = 2 * owner_ref[...]
    src_iota = lax.broadcasted_iota(jnp.int32, (128, CROSS), 0)
    of_src = (src_iota == csrc_ref[...]).astype(F32).astype(BF16)
    row_iota = lax.broadcasted_iota(jnp.int32, (256, 128), 0)
    perm0 = (row_iota == owner).astype(F32).astype(BF16)
    perm1 = (row_iota == owner + 1).astype(F32).astype(BF16)
    oh_t = jnp.concatenate([dot(perm0, of_src), dot(perm1, of_src)], axis=1)
    slots[:, 0:128] = oh_t.astype(BF16)
    slots[:, 128:256] = oh_t.astype(BF16)
    det_iota = lax.broadcasted_iota(jnp.int32, (ROWS, CROSS), 0)
    of_det = (det_iota == cdet_ref[...]).astype(F32).T.astype(BF16)
    dets[...] = jnp.concatenate([of_det, of_det], axis=1)
    start = jnp.broadcast_to(cstart_ref[...], (128, CROSS)).T
    first_tile[...] = start >> 7
    shift[...] = start & 127
    cnt[...] = jnp.broadcast_to(jnp.sum(oh_t, axis=1, keepdims=True), (256, 128)).reshape(DET, 8, 128)

    far_first = sorted(
        ((p, q) for p in range(RING) for q in range(RING) if p or q),
        key=lambda v: -(min(v[0], RING - v[0]) + min(v[1], RING - v[1])),
    )
    pl.semaphore_wait(ready_sem, len(lines))
    for s, (base, width, order) in enumerate(SETS):
        copies_c[s].wait_recv()
        span = pl.ds(base, RING * width)
        acc[:, :, span] += got_c[:, :, span]
        for k, (p, q) in enumerate(far_first):
            block = cols(base + lax.rem(coord[order[0]] + p, RING) * width, width)
            remote(
                acc.at[lax.rem(coord[order[1]] + q, RING), :, block], got_p.at[k, :, pl.ds(PLACE[s], width)],
                p_sem.at[s, 0], p_sem.at[s, 1], reach({order[0]: p, order[1]: q}),
            ).start()

    small[1].wait()
    line = jnp.concatenate([taps_ref[...], jnp.zeros((1, 256 - TAPS), F32)], axis=1)
    turned = pltpu.roll(jnp.broadcast_to(line, (128, 256)), 192, 1, stride=1, stride_axis=0)
    b_hi, b_lo = split(turned.T)
    band[:, 0:128] = b_hi
    band[:, 128:256] = b_lo

    def from_plane(s, rows, sems):
        every = got_p.at[:, 0:rows, pl.ds(PLACE[s], SETS[s][1])]
        return remote(every, every, sems.at[s, 0], sems.at[s, 1], partner)

    axis3 = []
    for s, (base, width, order) in enumerate(SETS):
        from_plane(s, 16, p_sem).wait_recv()
        span = pl.ds(PLACE[s], width)
        total = acc[coord[order[1]], :, cols(base + coord[order[0]] * width, width)]
        for k in range(len(far_first)):
            total += got_p[k, :, span]
        acc2[:, span] = total
        for step in range(1, RING):
            axis3.append(remote(
                acc2.at[:, span], got3.at[step - 1, :, span],
                r_sem.at[s, step - 1, 0], r_sem.at[s, step - 1, 1], reach({order[2]: step}),
            ))
            axis3[-1].start()

    copies_n = []
    for step in range(1, DET):
        to = lax.rem(det + step, DET)
        copies_n.append(
            remote(cnt.at[to], cnt_got.at[step - 1], t_sem.at[0], t_sem.at[1], (wafer, to))
        )
        copies_n[-1].start()

    for s, (base, width, order) in enumerate(SETS):
        for one in axis3[3 * s:3 * s + 3]:
            one.wait_recv()
        span = pl.ds(PLACE[s], width)
        whole = (acc2[:, span] + got3[0, :, span]) + (got3[1, :, span] + got3[2, :, span])
        block = cols(core * HALF + base + coord[order[0]] * width, width)
        amp[coord[order[1]], :, block] = whole[0:8] / (whole[8:16] + 1.0)
        here = amp.at[coord[order[1]], :, block]
        for p, q in far_first:
            remote(here, here, g_sem.at[s, 0], g_sem.at[s, 1], reach({order[0]: p, order[1]: q})).start()

    for edge in (res_hi, res_lo):
        edge[:, 0:128] = jnp.zeros((ROWS, 128), BF16)
        edge[:, 128 + NS:256 + NS] = jnp.zeros((ROWS, 128), BF16)

    def model_block(b, wide):
        span = cols(b * 512, 512)
        a_hi, a_lo = split(amp[:, :, span].reshape(MODES, 512))
        value = dot(lhs_m[...], jnp.concatenate([a_hi, a_hi, a_lo], axis=0))
        model[:, span] = value
        r_hi, r_lo = split(jnp.where(mask[:, span] != 0, tod[:, span] - value, 0.0))
        res_hi[:, cols(b * 512 + 128, 512)] = r_hi
        res_lo[:, cols(b * 512 + 128, 512)] = r_lo
        lines = dot(dets[...], jnp.concatenate([r_hi, r_lo], axis=0))
        tile = first_tile[...]
        wide = list(wide)
        for q in range(4):
            for w in range(3):
                wide[w] = jnp.where(tile == b * 4 + q - w, lines[:, 128 * q:128 * q + 128], wide[w])
        return tuple(wide)

    wide = (jnp.zeros((CROSS, 128), F32),) * 3
    copies_a = []
    for s, (base, width, _) in enumerate(SETS):
        from_plane(s, 8, g_sem).wait_recv()
        half = amp.at[:, :, cols(core * HALF + base, RING * width)]
        copies_a.append(remote(half, half, gc_sem.at[s, 0], gc_sem.at[s, 1], partner))
        copies_a[-1].start()
        first = core * (HALF // 512) + base // 512
        wide = lax.fori_loop(first, first + RING * width // 512, model_block, wide)
    for s, (base, width, _) in enumerate(SETS):
        copies_a[s].wait_recv()
        first = (1 - core) * (HALF // 512) + base // 512
        wide = lax.fori_loop(first, first + RING * width // 512, model_block, wide)

    rows = jnp.concatenate(wide, axis=1)
    rest = jnp.concatenate([shift[...]] * 3, axis=1)
    for bit in range(7):
        moved = pltpu.roll(rows, 384 - (1 << bit), 1)
        rows = jnp.where((rest & (1 << bit)) != 0, moved, rows)
    snip[0:CROSS, :] = rows[:, 0:128]
    snip[CROSS:2 * CROSS, :] = rows[:, 128:256]
    s_hi, s_lo = split(snip[...])
    tsum[...] = dot(slots[...], jnp.concatenate([s_hi, s_lo], axis=0)).reshape(DET, 8, 128)
    copies_t = []
    for step in range(1, DET):
        to = lax.rem(det + step, DET)
        copies_t.append(
            remote(tsum.at[to], tsum_got.at[step - 1], t_sem.at[2], t_sem.at[3], (wafer, to))
        )
        copies_t[-1].start()

    lane64 = lax.broadcasted_iota(jnp.int32, (ROWS, 128), 1) < 64

    def fill_block(b, carry):
        pieces = []
        for res in (res_hi, res_lo):
            left = []
            for q in range(4):
                before = res[:, cols(b * 512 + q * 128, 128)]
                here = res[:, cols(b * 512 + q * 128 + 128, 128)]
                after = res[:, cols(b * 512 + q * 128 + 256, 128)]
                left.append(jnp.concatenate([here, jnp.where(lane64, after, before)], axis=1))
            pieces.append(jnp.concatenate(left, axis=0))
        l_hi, l_lo = pieces
        first = dot(l_hi, band[...])
        second = dot(l_lo, band[:, 0:128])
        smooth = first[:, 0:128] + (first[:, 128:256] + second)
        for q in range(4):
            span = cols(b * 512 + q * 128, 128)
            filled[:, span] = jnp.where(
                mask[:, span] != 0, tod[:, span], model[:, span] + smooth[q * ROWS:(q + 1) * ROWS]
            )
        return carry

    outs = []
    for part_of in range(4):
        lax.fori_loop(part_of * 4, part_of * 4 + 4, fill_block, 0)
        span = pl.ds(part_of * 2048, 2048)
        outs.append(pltpu.make_async_copy(filled.at[:, span], filled_hbm.at[:, span], out_sem.at[part_of]))
        outs[-1].start()

    def wait_all(src, dst, send, recv):
        every = remote(src.at[0:DET - 1], dst.at[0:DET - 1], send, recv, partner)
        every.wait_recv()
        every.wait_send()

    wait_all(cnt, cnt_got, t_sem.at[0], t_sem.at[1])
    wait_all(tsum, tsum_got, t_sem.at[2], t_sem.at[3])
    number = cnt[det]
    total = tsum[det]
    for step in range(DET - 1):
        number += cnt_got[step]
        total += tsum_got[step]
    snip[0:8, :] = total / (number + 1.0)
    for o in range(4):
        templ_ref[0, o:o + 1, 0:128] = snip[2 * o:2 * o + 1, :]
        templ_ref[0, o:o + 1, 128:256] = snip[2 * o + 1:2 * o + 2, :]

    for one in outs:
        one.wait()
    for one in copies_c + copies_a + axis3:
        one.wait_send()
    for s in range(3):
        from_plane(s, 16, p_sem).wait_send()
        from_plane(s, 8, g_sem).wait_send()


def on_device(tod, gap_mask, coupling, taps, cross_det, cross_start, cross_src, src_owner):
    vmem, hbm = (pl.BlockSpec(memory_space=m) for m in (pltpu.VMEM, pltpu.HBM))
    return pl.pallas_call(
        kernel,
        out_shape=(
            jax.ShapeDtypeStruct((ROWS, NS), F32),
            jax.ShapeDtypeStruct((1, 4, 256), F32),
        ),
        in_specs=[hbm] * 8,
        out_specs=(hbm, vmem),
        scratch_shapes=[
            pltpu.VMEM((MODES, ROWS), F32),
            pltpu.VMEM((1, TAPS), F32),
            pltpu.VMEM((1, CROSS), jnp.int32),
            pltpu.VMEM((1, CROSS), jnp.int32),
            pltpu.VMEM((1, CROSS), jnp.int32),
            pltpu.VMEM((1, 128), jnp.int32),
            pltpu.VMEM((ROWS, NS), F32),
            pltpu.VMEM((ROWS, NS), F32),
            pltpu.VMEM((ROWS, NS), jnp.int32),
            pltpu.VMEM((ROWS, NS), F32),
            pltpu.VMEM((ROWS, NS + 256), BF16),
            pltpu.VMEM((ROWS, NS + 256), BF16),
            pltpu.VMEM((RING, 16, HALF), F32),
            pltpu.VMEM((RING, 16, HALF), F32),
            pltpu.VMEM((RING, 16, HALF), F32),
            pltpu.VMEM((RING * RING - 1, 16, BLOCKS), F32),
            pltpu.VMEM((16, BLOCKS), F32),
            pltpu.VMEM((3, 16, BLOCKS), F32),
            pltpu.VMEM((RING, 8, NS), F32),
            pltpu.VMEM((96, 256), BF16),
            pltpu.VMEM((ROWS, 96), BF16),
            pltpu.VMEM((256, 256), BF16),
            pltpu.VMEM((256, 256), BF16),
            pltpu.VMEM((CROSS, 128), BF16),
            pltpu.VMEM((CROSS, 128), jnp.int32),
            pltpu.VMEM((CROSS, 128), jnp.int32),
            pltpu.VMEM((2 * CROSS, 128), F32),
            pltpu.VMEM((DET, 8, 128), F32),
            pltpu.VMEM((DET, 8, 128), F32),
            pltpu.VMEM((DET, 8, 128), F32),
            pltpu.VMEM((DET, 8, 128), F32),
            pltpu.SemaphoreType.DMA((2, 3, 2)),
            pltpu.SemaphoreType.DMA((6,)),
            pltpu.SemaphoreType.DMA((4,)),
            pltpu.SemaphoreType.REGULAR,
            pltpu.SemaphoreType.DMA((3, 2)),
            pltpu.SemaphoreType.DMA((3, 2)),
            pltpu.SemaphoreType.DMA((3, 3, 2)),
            pltpu.SemaphoreType.DMA((3, 2)),
            pltpu.SemaphoreType.DMA((3, 2)),
            pltpu.SemaphoreType.DMA((4,)),
        ],
        compiler_params=pltpu.CompilerParams(
            collective_id=0, has_side_effects=True, vmem_limit_bytes=67043328
        ),
    )(tod, gap_mask, coupling.T, *(v.reshape(1, -1) for v in (taps, cross_det, cross_start, cross_src, src_owner)))


def solution(mesh):
    return jax.shard_map(
        on_device,
        mesh=mesh,
        in_specs=(
            P(("wafer", "det"), None),
            P(("wafer", "det"), None),
            P(("wafer", "det"), None),
            P(),
            P(("wafer", "det")),
            P(("wafer", "det")),
            P(("wafer", "det")),
            P(),
        ),
        out_specs=(P(("wafer", "det"), None), P("wafer", "det", None)),
        check_vma=False,
    )
```

```python
import functools

import jax
import jax.numpy as jnp
from jax import lax
from jax.experimental import pallas as pl
from jax.experimental.pallas import tpu as pltpu
from jax.sharding import PartitionSpec as P

MESH = pl.DeviceIdType.MESH
F32 = jnp.float32
BF16 = jnp.bfloat16

ROWS = 64
NS = 8192
HALF = NS // 2
MODES = 32
TAPS = 129
CROSS = 64
RING = 4
DET = 32
SETS = (
    (0, 384, ("x", "y", "z")),
    (1536, 384, ("y", "z", "x")),
    (3072, 256, ("z", "x", "y")),
)
PLACE = (0, 384, 768)
BLOCKS = 1024


def split(v):
    hi = v.astype(BF16)
    lo = (v - hi.astype(F32)).astype(BF16)
    return hi, lo


def dot(a, b):
    return jnp.dot(a, b, preferred_element_type=F32)


def kernel(
    tod_hbm, mask_hbm, coup_hbm, taps_hbm, cdet_hbm, cstart_hbm, csrc_hbm, owner_hbm,
    filled, templ_ref,
    coup_ref, taps_ref, cdet_ref, cstart_ref, csrc_ref, owner_ref,
    tod, mask, model, res_hi, res_lo,
    part, acc, got_c, got_p, acc2, got3, amp,
    lhs_p, lhs_m, band,
    slots, dets, first_tile, shift, tod_snip, good_snip, snip, cnt, cnt_got, tsum, tsum_got,
    in_sem, small_sem, ready_sem, c_sem, p_sem, r_sem, g_sem, gc_sem, t_sem,
):
    wafer = lax.axis_index("wafer")
    det = lax.axis_index("det")
    core = lax.rem(det, 2)
    x = lax.rem(lax.div(det, 2), RING)
    y = lax.div(det, 2 * RING)
    coord = {"x": x, "y": y, "z": wafer}

    def reach(steps):
        at = {a: lax.rem(coord[a] + steps[a], RING) if steps.get(a) else coord[a] for a in coord}
        return (at["z"], (at["y"] * RING + at["x"]) * 2 + core)

    partner = (wafer, det + 1 - 2 * core)

    def remote(src, dst, send, recv, to):
        return pltpu.make_async_remote_copy(
            src_ref=src, dst_ref=dst, send_sem=send, recv_sem=recv,
            device_id=to, device_id_type=MESH,
        )

    def cols(first, width):
        return pl.ds(pl.multiple_of(first, 128), width)

    small = []
    for k, (src, dst) in enumerate((
        (coup_hbm, coup_ref), (taps_hbm, taps_ref), (cdet_hbm, cdet_ref),
        (cstart_hbm, cstart_ref), (csrc_hbm, csrc_ref), (owner_hbm, owner_ref),
    )):
        small.append(pltpu.make_async_copy(src, dst, small_sem.at[k]))
        small[-1].start()

    halves = (1 - core, core)
    loads = []
    for h in range(2):
        for s, (base, width, _) in enumerate(SETS):
            span = cols(halves[h] * HALF + base, RING * width)
            pair = (
                pltpu.make_async_copy(tod_hbm.at[:, span], tod.at[:, span], in_sem.at[h, s, 0]),
                pltpu.make_async_copy(mask_hbm.at[:, span], mask.at[:, span], in_sem.at[h, s, 1]),
            )
            for one in pair:
                one.start()
            loads.append(pair)

    lines = [reach({a: step}) for a in ("x", "y", "z") for step in range(1, RING)]
    barrier = pltpu.get_barrier_semaphore()
    for to in [partner] + lines:
        pl.semaphore_signal(barrier, inc=1, device_id=to, device_id_type=MESH)

    small[0].wait()
    coup_t = coup_ref[...]
    c_hi, c_lo = split(coup_t.T)
    lhs_m[0:ROWS, :] = jnp.concatenate([c_hi, c_lo, c_hi], axis=1)
    t_hi, t_lo = split(coup_t)
    w_hi, w_lo = split(coup_t * coup_t)
    zero = jnp.zeros((MODES, ROWS), BF16)
    lhs_p[0:32, :] = jnp.concatenate([t_hi, t_lo, t_hi, zero], axis=1)
    lhs_p[32:64, :] = jnp.concatenate([zero, zero, zero, w_hi], axis=1)
    lhs_p[64:96, :] = jnp.concatenate([zero, zero, zero, w_lo], axis=1)

    def partial_sums(first, width):
        span = cols(first, width)
        m = mask[:, span]
        v = jnp.where(m != 0, tod[:, span], 0.0)
        v_hi, v_lo = split(v)
        g = m.astype(F32).astype(BF16)
        out = dot(lhs_p[...], jnp.concatenate([v_hi, v_hi, v_lo, g], axis=0))
        return out[0:32], out[32:64] + out[64:96]

    def fill(h, s, dst):
        base, width, _ = SETS[s]
        for one in loads[h * 3 + s]:
            one.wait()

        def body(i, carry):
            local = base + i * width
            sums, weights = partial_sums(halves[h] * HALF + local, width)
            span = cols(local, width)
            for j in range(RING):
                dst[j, 0:8, span] = sums[8 * j:8 * j + 8]
                dst[j, 8:16, span] = weights[8 * j:8 * j + 8]
            return carry

        lax.fori_loop(0, RING, body, 0)

    copies_c = []
    for s, (base, width, _) in enumerate(SETS):
        span = pl.ds(base, RING * width)
        copies_c.append(
            remote(part.at[:, :, span], got_c.at[:, :, span], c_sem.at[s, 0], c_sem.at[s, 1], partner)
        )
    for s in range(3):
        fill(0, s, part)
    pl.semaphore_wait(barrier, 1 + len(lines))
    for one in copies_c:
        one.start()
    for to in lines:
        pl.semaphore_signal(ready_sem, inc=1, device_id=to, device_id_type=MESH)

    steps = sorted(
        ((p, q) for p in range(RING) for q in range(RING) if p or q),
        key=lambda v: -(min(v[0], RING - v[0]) + min(v[1], RING - v[1])),
    )
    on_line = [v for v in steps if not (v[0] and v[1])]
    off_line = [v for v in steps if v[0] and v[1]]

    def scatter(s, which):
        base, width, order = SETS[s]
        for p, q in which:
            block = cols(base + lax.rem(coord[order[0]] + p, RING) * width, width)
            remote(
                acc.at[lax.rem(coord[order[1]] + q, RING), :, block],
                got_p.at[steps.index((p, q)), :, pl.ds(PLACE[s], width)],
                p_sem.at[s, 0], p_sem.at[s, 1], reach({order[0]: p, order[1]: q}),
            ).start()

    for s, (base, width, order) in enumerate(SETS):
        fill(1, s, acc)
        copies_c[s].wait_recv()
        span = pl.ds(base, RING * width)
        acc[:, :, span] += got_c[:, :, span]
        if s == 0:
            scatter(s, on_line)
            pl.semaphore_wait(ready_sem, len(lines))
            scatter(s, off_line)
        else:
            scatter(s, steps)

    for one in small[2:]:
        one.wait()
    owner = 2 * owner_ref[...]
    src_iota = lax.broadcasted_iota(jnp.int32, (128, CROSS), 0)
    of_src = (src_iota == csrc_ref[...]).astype(F32).astype(BF16)
    row_iota = lax.broadcasted_iota(jnp.int32, (256, 128), 0)
    perm0 = (row_iota == owner).astype(F32).astype(BF16)
    perm1 = (row_iota == owner + 1).astype(F32).astype(BF16)
    oh_t = jnp.concatenate([dot(perm0, of_src), dot(perm1, of_src)], axis=1)
    slots[:, 0:128] = oh_t.astype(BF16)
    slots[:, 128:256] = oh_t.astype(BF16)
    det_iota = lax.broadcasted_iota(jnp.int32, (ROWS, CROSS), 0)
    of_det = (det_iota == cdet_ref[...]).astype(F32).T.astype(BF16)
    dets[...] = jnp.concatenate([of_det, of_det], axis=1)
    start = jnp.broadcast_to(cstart_ref[...], (128, CROSS)).T
    first_tile[...] = start >> 7
    shift[...] = start & 127
    lhs_m[ROWS:ROWS + CROSS, :] = dot(of_det, lhs_m[0:ROWS, :]).astype(BF16)
    cnt[...] = jnp.broadcast_to(jnp.sum(oh_t, axis=1, keepdims=True), (256, 128)).reshape(DET, 8, 128)

    small[1].wait()
    line = jnp.concatenate([taps_ref[...], jnp.zeros((1, 256 - TAPS), F32)], axis=1)
    turned = pltpu.roll(jnp.broadcast_to(line, (128, 256)), 192, 1, stride=1, stride_axis=0)
    b_hi, b_lo = split(turned.T)
    band[:, 0:128] = b_hi
    band[:, 128:256] = b_lo

    def choose(b, lines, wide):
        tile = first_tile[...]
        at = {v: tile == b * 4 + v for v in range(-2, 4)}
        wide = list(wide)
        for q in range(4):
            for w in range(3):
                wide[w] = jnp.where(at[q - w], lines[:, 128 * q:128 * q + 128], wide[w])
        return tuple(wide)

    def shifted(wide):
        rows = jnp.concatenate(wide, axis=1)
        rest = jnp.concatenate([shift[...]] * 3, axis=1)
        for bit in range(7):
            moved = pltpu.roll(rows, 384 - (1 << bit), 1)
            rows = jnp.where((rest & (1 << bit)) != 0, moved, rows)
        return rows[:, 0:256]

    no_tiles = (jnp.zeros((CROSS, 128), F32),) * 3

    def tod_block(b, wide):
        span = cols(b * 512, 512)
        v_hi, v_lo = split(jnp.where(mask[:, span] != 0, tod[:, span], 0.0))
        return choose(b, dot(dets[...], jnp.concatenate([v_hi, v_lo], axis=0)), wide)

    def good_block(b, wide):
        g = mask[:, cols(b * 512, 512)].astype(F32).astype(BF16)
        return choose(b, dot(dets[:, 0:ROWS], g), wide)

    tod_snip[...] = shifted(lax.fori_loop(0, NS // 512, tod_block, no_tiles))
    good_snip[...] = shifted(lax.fori_loop(0, NS // 512, good_block, no_tiles))
    for edge in (res_hi, res_lo):
        edge[:, 0:128] = jnp.zeros((ROWS, 128), BF16)
        edge[:, 128 + NS:256 + NS] = jnp.zeros((ROWS, 128), BF16)

    def from_plane(s, rows, sems):
        every = got_p.at[:, 0:rows, pl.ds(PLACE[s], SETS[s][1])]
        return remote(every, every, sems.at[s, 0], sems.at[s, 1], partner)

    axis3 = []
    for s, (base, width, order) in enumerate(SETS):
        from_plane(s, 16, p_sem).wait_recv()
        span = pl.ds(PLACE[s], width)
        total = acc[coord[order[1]], :, cols(base + coord[order[0]] * width, width)]
        for k in range(len(steps)):
            total += got_p[k, :, span]
        acc2[:, span] = total
        for step in range(1, RING):
            axis3.append(remote(
                acc2.at[:, span], got3.at[step - 1, :, span],
                r_sem.at[s, step - 1, 0], r_sem.at[s, step - 1, 1], reach({order[2]: step}),
            ))
            axis3[-1].start()

    copies_n = []
    for step in range(1, DET):
        to = lax.rem(det + step, DET)
        copies_n.append(
            remote(cnt.at[to], cnt_got.at[step - 1], t_sem.at[0], t_sem.at[1], (wafer, to))
        )
        copies_n[-1].start()

    for s, (base, width, order) in enumerate(SETS):
        for one in axis3[3 * s:3 * s + 3]:
            one.wait_recv()
        span = pl.ds(PLACE[s], width)
        whole = (acc2[:, span] + got3[0, :, span]) + (got3[1, :, span] + got3[2, :, span])
        block = cols(core * HALF + base + coord[order[0]] * width, width)
        amp[coord[order[1]], :, block] = whole[0:8] / (whole[8:16] + 1.0)
        here = amp.at[coord[order[1]], :, block]
        for p, q in steps:
            remote(here, here, g_sem.at[s, 0], g_sem.at[s, 1], reach({order[0]: p, order[1]: q})).start()

    def model_block(b, wide):
        span = cols(b * 512, 512)
        a_hi, a_lo = split(amp[:, :, span].reshape(MODES, 512))
        value = dot(lhs_m[...], jnp.concatenate([a_hi, a_hi, a_lo], axis=0))
        model[:, span] = value[0:ROWS]
        return choose(b, value[ROWS:ROWS + CROSS], wide)

    wide = no_tiles
    copies_a = []
    for s, (base, width, _) in enumerate(SETS):
        from_plane(s, 8, g_sem).wait_recv()
        half = amp.at[:, :, cols(core * HALF + base, RING * width)]
        copies_a.append(remote(half, half, gc_sem.at[s, 0], gc_sem.at[s, 1], partner))
        copies_a[-1].start()
        first = core * (HALF // 512) + base // 512
        wide = lax.fori_loop(first, first + RING * width // 512, model_block, wide)
    for s, (base, width, _) in enumerate(SETS):
        copies_a[s].wait_recv()
        first = (1 - core) * (HALF // 512) + base // 512
        wide = lax.fori_loop(first, first + RING * width // 512, model_block, wide)

    rows = jnp.where(good_snip[...] != 0.0, tod_snip[...] - shifted(wide), 0.0)
    snip[0:CROSS, :] = rows[:, 0:128]
    snip[CROSS:2 * CROSS, :] = rows[:, 128:256]
    s_hi, s_lo = split(snip[...])
    tsum[...] = dot(slots[...], jnp.concatenate([s_hi, s_lo], axis=0)).reshape(DET, 8, 128)
    copies_t = []
    for step in range(1, DET):
        to = lax.rem(det + step, DET)
        copies_t.append(
            remote(tsum.at[to], tsum_got.at[step - 1], t_sem.at[2], t_sem.at[3], (wafer, to))
        )
        copies_t[-1].start()

    def resid_block(b, carry):
        span = cols(b * 512, 512)
        r_hi, r_lo = split(jnp.where(mask[:, span] != 0, tod[:, span] - model[:, span], 0.0))
        res_hi[:, cols(b * 512 + 128, 512)] = r_hi
        res_lo[:, cols(b * 512 + 128, 512)] = r_lo
        return carry

    lax.fori_loop(0, NS // 512, resid_block, 0)
    lane64 = lax.broadcasted_iota(jnp.int32, (ROWS, 128), 1) < 64

    def fill_block(b, carry):
        pieces = []
        for res in (res_hi, res_lo):
            left = []
            for q in range(4):
                before = res[:, cols(b * 512 + q * 128, 128)]
                here = res[:, cols(b * 512 + q * 128 + 128, 128)]
                after = res[:, cols(b * 512 + q * 128 + 256, 128)]
                left.append(jnp.concatenate([here, jnp.where(lane64, after, before)], axis=1))
            pieces.append(jnp.concatenate(left, axis=0))
        l_hi, l_lo = pieces
        first = dot(l_hi, band[...])
        second = dot(l_lo, band[:, 0:128])
        smooth = first[:, 0:128] + (first[:, 128:256] + second)
        for q in range(4):
            span = cols(b * 512 + q * 128, 128)
            filled[:, span] = jnp.where(
                mask[:, span] != 0, tod[:, span], model[:, span] + smooth[q * ROWS:(q + 1) * ROWS]
            )
        return carry

    lax.fori_loop(0, NS // 512, fill_block, 0)

    def wait_all(src, dst, send, recv):
        every = remote(src.at[0:DET - 1], dst.at[0:DET - 1], send, recv, partner)
        every.wait_recv()
        every.wait_send()

    wait_all(cnt, cnt_got, t_sem.at[0], t_sem.at[1])
    wait_all(tsum, tsum_got, t_sem.at[2], t_sem.at[3])
    number = cnt[det]
    total = tsum[det]
    for step in range(DET - 1):
        number += cnt_got[step]
        total += tsum_got[step]
    snip[0:8, :] = total / (number + 1.0)
    for o in range(4):
        templ_ref[0, o:o + 1, 0:128] = snip[2 * o:2 * o + 1, :]
        templ_ref[0, o:o + 1, 128:256] = snip[2 * o + 1:2 * o + 2, :]

    for one in copies_c + copies_a + axis3:
        one.wait_send()
    for s in range(3):
        from_plane(s, 16, p_sem).wait_send()
        from_plane(s, 8, g_sem).wait_send()


def hand_out(filled, templ, filled_out, templ_out, sem):
    copies = [
        pltpu.make_async_copy(filled, filled_out, sem.at[0]),
        pltpu.make_async_copy(templ, templ_out, sem.at[1]),
    ]
    for one in copies:
        one.start()
    for one in copies:
        one.wait()


def on_device(tod, gap_mask, coupling, taps, cross_det, cross_start, cross_src, src_owner):
    vmem, hbm = (pl.BlockSpec(memory_space=m) for m in (pltpu.VMEM, pltpu.HBM))
    shapes = (jax.ShapeDtypeStruct((ROWS, NS), F32), jax.ShapeDtypeStruct((1, 4, 256), F32))
    results = pl.pallas_call(
        kernel,
        out_shape=shapes,
        in_specs=[hbm] * 8,
        out_specs=(vmem, vmem),
        scratch_shapes=[
            pltpu.VMEM((MODES, ROWS), F32),
            pltpu.VMEM((1, TAPS), F32),
            pltpu.VMEM((1, CROSS), jnp.int32),
            pltpu.VMEM((1, CROSS), jnp.int32),
            pltpu.VMEM((1, CROSS), jnp.int32),
            pltpu.VMEM((1, 128), jnp.int32),
            pltpu.VMEM((ROWS, NS), F32),
            pltpu.VMEM((ROWS, NS), jnp.int32),
            pltpu.VMEM((ROWS, NS), F32),
            pltpu.VMEM((ROWS, NS + 256), BF16),
            pltpu.VMEM((ROWS, NS + 256), BF16),
            pltpu.VMEM((RING, 16, HALF), F32),
            pltpu.VMEM((RING, 16, HALF), F32),
            pltpu.VMEM((RING, 16, HALF), F32),
            pltpu.VMEM((RING * RING - 1, 16, BLOCKS), F32),
            pltpu.VMEM((16, BLOCKS), F32),
            pltpu.VMEM((3, 16, BLOCKS), F32),
            pltpu.VMEM((RING, 8, NS), F32),
            pltpu.VMEM((96, 256), BF16),
            pltpu.VMEM((ROWS + CROSS, 96), BF16),
            pltpu.VMEM((256, 256), BF16),
            pltpu.VMEM((256, 256), BF16),
            pltpu.VMEM((CROSS, 128), BF16),
            pltpu.VMEM((CROSS, 128), jnp.int32),
            pltpu.VMEM((CROSS, 128), jnp.int32),
            pltpu.VMEM((CROSS, 256), F32),
            pltpu.VMEM((CROSS, 256), F32),
            pltpu.VMEM((2 * CROSS, 128), F32),
            pltpu.VMEM((DET, 8, 128), F32),
            pltpu.VMEM((DET, 8, 128), F32),
            pltpu.VMEM((DET, 8, 128), F32),
            pltpu.VMEM((DET, 8, 128), F32),
            pltpu.SemaphoreType.DMA((2, 3, 2)),
            pltpu.SemaphoreType.DMA((6,)),
            pltpu.SemaphoreType.REGULAR,
            pltpu.SemaphoreType.DMA((3, 2)),
            pltpu.SemaphoreType.DMA((3, 2)),
            pltpu.SemaphoreType.DMA((3, 3, 2)),
            pltpu.SemaphoreType.DMA((3, 2)),
            pltpu.SemaphoreType.DMA((3, 2)),
            pltpu.SemaphoreType.DMA((4,)),
        ],
        compiler_params=pltpu.CompilerParams(
            collective_id=0, has_side_effects=True, vmem_limit_bytes=40 << 20
        ),
    )(*(pltpu.with_memory_space_constraint(v, pltpu.HBM) for v in (tod, gap_mask, coupling.T, *(v.reshape(1, -1) for v in (taps, cross_det, cross_start, cross_src, src_owner)))))

    return pl.pallas_call(
        hand_out,
        out_shape=shapes,
        in_specs=[vmem] * 2,
        out_specs=(hbm, hbm),
        scratch_shapes=[pltpu.SemaphoreType.DMA((2,))],
        compiler_params=pltpu.CompilerParams(vmem_limit_bytes=1 << 20),
    )(*results)


def solution(mesh):
    return jax.shard_map(
        on_device,
        mesh=mesh,
        in_specs=(
            P(("wafer", "det"), None),
            P(("wafer", "det"), None),
            P(("wafer", "det"), None),
            P(),
            P(("wafer", "det")),
            P(("wafer", "det")),
            P(("wafer", "det")),
            P(),
        ),
        out_specs=(P(("wafer", "det"), None), P("wafer", "det", None)),
        check_vma=False,
    )
```

```python
import functools

import jax
import jax.numpy as jnp
from jax import lax
from jax.experimental import pallas as pl
from jax.experimental.pallas import tpu as pltpu
from jax.sharding import PartitionSpec as P

MESH = pl.DeviceIdType.MESH
F32 = jnp.float32
BF16 = jnp.bfloat16

ROWS = 64
NS = 8192
HALF = NS // 2
MODES = 32
TAPS = 129
CROSS = 64
RING = 4
DET = 32
SETS = (
    (0, 256, ("x", "y", "z")),
    (1024, 128, ("y", "z", "x")),
    (1536, 128, ("z", "x", "y")),
    (2048, 128, ("x", "y", "z")),
    (2560, 256, ("y", "z", "x")),
    (3584, 128, ("z", "x", "y")),
)
GROUPS = ((0, 1, 2), (3, 4, 5))
WIDE = HALF // len(GROUPS)
CHUNK = 512
PLACE = (0, 256, 384, 512, 640, 896)
BLOCKS = 1024


def split(v):
    hi = v.astype(BF16)
    lo = (v - hi.astype(F32)).astype(BF16)
    return hi, lo


def dot(a, b):
    return jnp.dot(a, b, preferred_element_type=F32)


def kernel(
    tod_hbm, mask_hbm, coup_hbm, taps_hbm, cdet_hbm, cstart_hbm, csrc_hbm, owner_hbm,
    filled, templ_ref,
    coup_ref, taps_ref, cdet_ref, cstart_ref, csrc_ref, owner_ref,
    tod, mask, model, res_hi, res_lo,
    part, acc, got_c, got_p, acc2, got3, amp,
    lhs_p, lhs_m, band,
    slots, dets, first_tile, shift, tod_snip, good_snip, snip, cnt, cnt_got, tsum, tsum_got,
    in_sem, small_sem, ready_sem, c_sem, p_sem, r_sem, g_sem, gc_sem, t_sem,
):
    wafer = lax.axis_index("wafer")
    det = lax.axis_index("det")
    core = lax.rem(det, 2)
    x = lax.rem(lax.div(det, 2), RING)
    y = lax.div(det, 2 * RING)
    coord = {"x": x, "y": y, "z": wafer}

    def reach(steps):
        at = {a: lax.rem(coord[a] + steps[a], RING) if steps.get(a) else coord[a] for a in coord}
        return (at["z"], (at["y"] * RING + at["x"]) * 2 + core)

    partner = (wafer, det + 1 - 2 * core)

    def remote(src, dst, send, recv, to):
        return pltpu.make_async_remote_copy(
            src_ref=src, dst_ref=dst, send_sem=send, recv_sem=recv,
            device_id=to, device_id_type=MESH,
        )

    def cols(first, width):
        return pl.ds(pl.multiple_of(first, 128), width)

    small = []
    for k, (src, dst) in enumerate((
        (coup_hbm, coup_ref), (taps_hbm, taps_ref), (cdet_hbm, cdet_ref),
        (cstart_hbm, cstart_ref), (csrc_hbm, csrc_ref), (owner_hbm, owner_ref),
    )):
        small.append(pltpu.make_async_copy(src, dst, small_sem.at[k]))
        small[-1].start()

    halves = (1 - core, core)
    loads = {}
    for h in range(2):
        for g in range(len(GROUPS)):
            span = cols(halves[h] * HALF + g * WIDE, WIDE)
            loads[h, g] = (
                pltpu.make_async_copy(tod_hbm.at[:, span], tod.at[:, span], in_sem.at[h, g, 0]),
                pltpu.make_async_copy(mask_hbm.at[:, span], mask.at[:, span], in_sem.at[h, g, 1]),
            )
            for one in loads[h, g]:
                one.start()

    lines = [reach({a: step}) for a in ("x", "y", "z") for step in range(1, RING)]
    barrier = pltpu.get_barrier_semaphore()
    for to in [partner] + lines:
        pl.semaphore_signal(barrier, inc=1, device_id=to, device_id_type=MESH)

    small[0].wait()
    coup_t = coup_ref[...]
    c_hi, c_lo = split(coup_t.T)
    lhs_m[0:ROWS, :] = jnp.concatenate([c_hi, c_lo, c_hi], axis=1)
    t_hi, t_lo = split(coup_t)
    w_hi, w_lo = split(coup_t * coup_t)
    zero = jnp.zeros((MODES, ROWS), BF16)
    lhs_p[0:32, :] = jnp.concatenate([t_hi, t_lo, t_hi, zero], axis=1)
    lhs_p[32:64, :] = jnp.concatenate([zero, zero, zero, w_hi], axis=1)
    lhs_p[64:96, :] = jnp.concatenate([zero, zero, zero, w_lo], axis=1)

    def partial_sums(first, width):
        span = cols(first, width)
        m = mask[:, span]
        v = jnp.where(m != 0, tod[:, span], 0.0)
        v_hi, v_lo = split(v)
        g = m.astype(F32).astype(BF16)
        out = dot(lhs_p[...], jnp.concatenate([v_hi, v_hi, v_lo, g], axis=0))
        return out[0:32], out[32:64] + out[64:96]

    def fill(h, g, dst):
        for one in loads[h, g]:
            one.wait()

        def body(i, carry):
            local = g * WIDE + i * CHUNK
            sums, weights = partial_sums(halves[h] * HALF + local, CHUNK)
            span = cols(local, CHUNK)
            for j in range(RING):
                dst[j, 0:8, span] = sums[8 * j:8 * j + 8]
                dst[j, 8:16, span] = weights[8 * j:8 * j + 8]
            return carry

        lax.fori_loop(0, WIDE // CHUNK, body, 0)

    copies_c = []
    for g in range(len(GROUPS)):
        span = pl.ds(g * WIDE, WIDE)
        copies_c.append(
            remote(part.at[:, :, span], got_c.at[:, :, span], c_sem.at[g, 0], c_sem.at[g, 1], partner)
        )
    fill(0, 0, part)
    fill(0, 1, part)
    pl.semaphore_wait(barrier, 1 + len(lines))
    copies_c[0].start()
    for to in lines:
        pl.semaphore_signal(ready_sem, inc=1, device_id=to, device_id_type=MESH)
    fill(1, 0, acc)
    copies_c[1].start()

    steps = sorted(
        ((p, q) for p in range(RING) for q in range(RING) if p or q),
        key=lambda v: -(min(v[0], RING - v[0]) + min(v[1], RING - v[1])),
    )
    on_line = [v for v in steps if not (v[0] and v[1])]
    off_line = [v for v in steps if v[0] and v[1]]

    def scatter(s, which):
        base, width, order = SETS[s]
        for p, q in which:
            block = cols(base + lax.rem(coord[order[0]] + p, RING) * width, width)
            remote(
                acc.at[lax.rem(coord[order[1]] + q, RING), :, block],
                got_p.at[steps.index((p, q)), :, pl.ds(PLACE[s], width)],
                p_sem.at[s, 0], p_sem.at[s, 1], reach({order[0]: p, order[1]: q}),
            ).start()

    def take(g):
        copies_c[g].wait_recv()
        span = pl.ds(g * WIDE, WIDE)
        acc[:, :, span] += got_c[:, :, span]

    take(0)
    for s in GROUPS[0]:
        scatter(s, on_line)
    pl.semaphore_wait(ready_sem, len(lines))
    for s in GROUPS[0]:
        scatter(s, off_line)
    fill(1, 1, acc)
    take(1)
    for s in GROUPS[1]:
        scatter(s, steps)

    for one in small[2:]:
        one.wait()
    owner = 2 * owner_ref[...]
    src_iota = lax.broadcasted_iota(jnp.int32, (128, CROSS), 0)
    of_src = (src_iota == csrc_ref[...]).astype(F32).astype(BF16)
    row_iota = lax.broadcasted_iota(jnp.int32, (256, 128), 0)
    perm0 = (row_iota == owner).astype(F32).astype(BF16)
    perm1 = (row_iota == owner + 1).astype(F32).astype(BF16)
    oh_t = jnp.concatenate([dot(perm0, of_src), dot(perm1, of_src)], axis=1)
    slots[:, 0:128] = oh_t.astype(BF16)
    slots[:, 128:256] = oh_t.astype(BF16)
    det_iota = lax.broadcasted_iota(jnp.int32, (ROWS, CROSS), 0)
    of_det = (det_iota == cdet_ref[...]).astype(F32).T.astype(BF16)
    dets[...] = jnp.concatenate([of_det, of_det], axis=1)
    start = jnp.broadcast_to(cstart_ref[...], (128, CROSS)).T
    first_tile[...] = start >> 7
    shift[...] = start & 127
    lhs_m[ROWS:ROWS + CROSS, :] = dot(of_det, lhs_m[0:ROWS, :]).astype(BF16)
    cnt[...] = jnp.broadcast_to(jnp.sum(oh_t, axis=1, keepdims=True), (256, 128)).reshape(DET, 8, 128)

    small[1].wait()
    line = jnp.concatenate([taps_ref[...], jnp.zeros((1, 256 - TAPS), F32)], axis=1)
    turned = pltpu.roll(jnp.broadcast_to(line, (128, 256)), 192, 1, stride=1, stride_axis=0)
    b_hi, b_lo = split(turned.T)
    band[:, 0:128] = b_hi
    band[:, 128:256] = b_lo

    def choose(b, lines, wide):
        tile = first_tile[...]
        at = {v: tile == b * 4 + v for v in range(-2, 4)}
        wide = list(wide)
        for q in range(4):
            for w in range(3):
                wide[w] = jnp.where(at[q - w], lines[:, 128 * q:128 * q + 128], wide[w])
        return tuple(wide)

    def shifted(wide):
        rows = jnp.concatenate(wide, axis=1)
        rest = jnp.concatenate([shift[...]] * 3, axis=1)
        for bit in range(7):
            moved = pltpu.roll(rows, 384 - (1 << bit), 1)
            rows = jnp.where((rest & (1 << bit)) != 0, moved, rows)
        return rows[:, 0:256]

    no_tiles = (jnp.zeros((CROSS, 128), F32),) * 3

    def tod_block(b, wide):
        span = cols(b * 512, 512)
        v_hi, v_lo = split(jnp.where(mask[:, span] != 0, tod[:, span], 0.0))
        return choose(b, dot(dets[...], jnp.concatenate([v_hi, v_lo], axis=0)), wide)

    def good_block(b, wide):
        g = mask[:, cols(b * 512, 512)].astype(F32).astype(BF16)
        return choose(b, dot(dets[:, 0:ROWS], g), wide)

    tod_snip[...] = shifted(lax.fori_loop(0, NS // 512, tod_block, no_tiles))
    for edge in (res_hi, res_lo):
        edge[:, 0:128] = jnp.zeros((ROWS, 128), BF16)
        edge[:, 128 + NS:256 + NS] = jnp.zeros((ROWS, 128), BF16)

    def from_plane(s, rows, sems):
        every = got_p.at[:, 0:rows, pl.ds(PLACE[s], SETS[s][1])]
        return remote(every, every, sems.at[s, 0], sems.at[s, 1], partner)

    axis3 = []
    for s, (base, width, order) in enumerate(SETS):
        if s == GROUPS[1][0]:
            good_snip[...] = shifted(lax.fori_loop(0, NS // 512, good_block, no_tiles))
        from_plane(s, 16, p_sem).wait_recv()
        span = pl.ds(PLACE[s], width)
        total = acc[coord[order[1]], :, cols(base + coord[order[0]] * width, width)]
        for k in range(len(steps)):
            total += got_p[k, :, span]
        acc2[:, span] = total
        for step in range(1, RING):
            axis3.append(remote(
                acc2.at[:, span], got3.at[step - 1, :, span],
                r_sem.at[s, step - 1, 0], r_sem.at[s, step - 1, 1], reach({order[2]: step}),
            ))
            axis3[-1].start()

    for s, (base, width, order) in enumerate(SETS):
        for one in axis3[3 * s:3 * s + 3]:
            one.wait_recv()
        span = pl.ds(PLACE[s], width)
        whole = (acc2[:, span] + got3[0, :, span]) + (got3[1, :, span] + got3[2, :, span])
        block = cols(core * HALF + base + coord[order[0]] * width, width)
        amp[coord[order[1]], :, block] = whole[0:8] / (whole[8:16] + 1.0)
        here = amp.at[coord[order[1]], :, block]
        for p, q in steps:
            remote(here, here, g_sem.at[s, 0], g_sem.at[s, 1], reach({order[0]: p, order[1]: q})).start()

    def send_counts():
        for step in range(1, DET):
            to = lax.rem(det + step, DET)
            remote(cnt.at[to], cnt_got.at[step - 1], t_sem.at[0], t_sem.at[1], (wafer, to)).start()

    def model_block(b, wide):
        span = cols(b * 512, 512)
        a_hi, a_lo = split(amp[:, :, span].reshape(MODES, 512))
        value = dot(lhs_m[...], jnp.concatenate([a_hi, a_hi, a_lo], axis=0))
        model[:, span] = value[0:ROWS]
        return choose(b, value[ROWS:ROWS + CROSS], wide)

    def resid_blocks(side, g):
        for b in range(WIDE // CHUNK):
            first = side * HALF + g * WIDE + b * CHUNK
            span = cols(first, CHUNK)
            r_hi, r_lo = split(jnp.where(mask[:, span] != 0, tod[:, span] - model[:, span], 0.0))
            res_hi[:, cols(first + 128, CHUNK)] = r_hi
            res_lo[:, cols(first + 128, CHUNK)] = r_lo

    def model_blocks(side, g, wide):
        for b in range(WIDE // CHUNK):
            wide = model_block((side * HALF + g * WIDE) // CHUNK + b, wide)
        return wide

    wide = no_tiles
    copies_a = []
    for g, members in enumerate(GROUPS):
        for s in members:
            from_plane(s, 8, g_sem).wait_recv()
        half = amp.at[:, :, cols(core * HALF + g * WIDE, WIDE)]
        copies_a.append(remote(half, half, gc_sem.at[g, 0], gc_sem.at[g, 1], partner))
        copies_a[g].start()
        if g == len(GROUPS) - 1:
            send_counts()
        wide = model_blocks(core, g, wide)
        resid_blocks(core, g)
        if g > 0:
            resid_blocks(1 - core, g - 1)
        copies_a[g].wait_recv()
        wide = model_blocks(1 - core, g, wide)

    rows = jnp.where(good_snip[...] != 0.0, tod_snip[...] - shifted(wide), 0.0)
    snip[0:CROSS, :] = rows[:, 0:128]
    snip[CROSS:2 * CROSS, :] = rows[:, 128:256]
    s_hi, s_lo = split(snip[...])
    tsum[...] = dot(slots[...], jnp.concatenate([s_hi, s_lo], axis=0)).reshape(DET, 8, 128)
    copies_t = []
    for step in range(1, DET):
        to = lax.rem(det + step, DET)
        copies_t.append(
            remote(tsum.at[to], tsum_got.at[step - 1], t_sem.at[2], t_sem.at[3], (wafer, to))
        )
        copies_t[-1].start()

    resid_blocks(1 - core, len(GROUPS) - 1)
    lane64 = lax.broadcasted_iota(jnp.int32, (ROWS, 128), 1) < 64

    def fill_block(b, carry):
        pieces = []
        for res in (res_hi, res_lo):
            left = []
            for q in range(4):
                before = res[:, cols(b * 512 + q * 128, 128)]
                here = res[:, cols(b * 512 + q * 128 + 128, 128)]
                after = res[:, cols(b * 512 + q * 128 + 256, 128)]
                left.append(jnp.concatenate([here, jnp.where(lane64, after, before)], axis=1))
            pieces.append(jnp.concatenate(left, axis=0))
        l_hi, l_lo = pieces
        first = dot(l_hi, band[...])
        second = dot(l_lo, band[:, 0:128])
        smooth = first[:, 0:128] + (first[:, 128:256] + second)
        for q in range(4):
            span = cols(b * 512 + q * 128, 128)
            filled[:, span] = jnp.where(
                mask[:, span] != 0, tod[:, span], model[:, span] + smooth[q * ROWS:(q + 1) * ROWS]
            )
        return carry

    lax.fori_loop(0, NS // 512, fill_block, 0)

    def wait_all(src, dst, send, recv):
        every = remote(src.at[0:DET - 1], dst.at[0:DET - 1], send, recv, partner)
        every.wait_recv()
        every.wait_send()

    wait_all(cnt, cnt_got, t_sem.at[0], t_sem.at[1])
    wait_all(tsum, tsum_got, t_sem.at[2], t_sem.at[3])
    number = cnt[det]
    total = tsum[det]
    for step in range(DET - 1):
        number += cnt_got[step]
        total += tsum_got[step]
    snip[0:8, :] = total / (number + 1.0)
    for o in range(4):
        templ_ref[0, o:o + 1, 0:128] = snip[2 * o:2 * o + 1, :]
        templ_ref[0, o:o + 1, 128:256] = snip[2 * o + 1:2 * o + 2, :]

    for one in copies_c + copies_a + axis3:
        one.wait_send()
    for s in range(len(SETS)):
        from_plane(s, 16, p_sem).wait_send()
        from_plane(s, 8, g_sem).wait_send()


def hand_out(filled, templ, filled_out, templ_out, sem):
    copies = [
        pltpu.make_async_copy(filled, filled_out, sem.at[0]),
        pltpu.make_async_copy(templ, templ_out, sem.at[1]),
    ]
    for one in copies:
        one.start()
    for one in copies:
        one.wait()


def on_device(tod, gap_mask, coupling, taps, cross_det, cross_start, cross_src, src_owner):
    vmem, hbm = (pl.BlockSpec(memory_space=m) for m in (pltpu.VMEM, pltpu.HBM))
    shapes = (jax.ShapeDtypeStruct((ROWS, NS), F32), jax.ShapeDtypeStruct((1, 4, 256), F32))
    results = pl.pallas_call(
        kernel,
        out_shape=shapes,
        in_specs=[hbm] * 8,
        out_specs=(vmem, vmem),
        scratch_shapes=[
            pltpu.VMEM((MODES, ROWS), F32),
            pltpu.VMEM((1, TAPS), F32),
            pltpu.VMEM((1, CROSS), jnp.int32),
            pltpu.VMEM((1, CROSS), jnp.int32),
            pltpu.VMEM((1, CROSS), jnp.int32),
            pltpu.VMEM((1, 128), jnp.int32),
            pltpu.VMEM((ROWS, NS), F32),
            pltpu.VMEM((ROWS, NS), jnp.int32),
            pltpu.VMEM((ROWS, NS), F32),
            pltpu.VMEM((ROWS, NS + 256), BF16),
            pltpu.VMEM((ROWS, NS + 256), BF16),
            pltpu.VMEM((RING, 16, HALF), F32),
            pltpu.VMEM((RING, 16, HALF), F32),
            pltpu.VMEM((RING, 16, HALF), F32),
            pltpu.VMEM((RING * RING - 1, 16, BLOCKS), F32),
            pltpu.VMEM((16, BLOCKS), F32),
            pltpu.VMEM((3, 16, BLOCKS), F32),
            pltpu.VMEM((RING, 8, NS), F32),
            pltpu.VMEM((96, 256), BF16),
            pltpu.VMEM((ROWS + CROSS, 96), BF16),
            pltpu.VMEM((256, 256), BF16),
            pltpu.VMEM((256, 256), BF16),
            pltpu.VMEM((CROSS, 128), BF16),
            pltpu.VMEM((CROSS, 128), jnp.int32),
            pltpu.VMEM((CROSS, 128), jnp.int32),
            pltpu.VMEM((CROSS, 256), F32),
            pltpu.VMEM((CROSS, 256), F32),
            pltpu.VMEM((2 * CROSS, 128), F32),
            pltpu.VMEM((DET, 8, 128), F32),
            pltpu.VMEM((DET, 8, 128), F32),
            pltpu.VMEM((DET, 8, 128), F32),
            pltpu.VMEM((DET, 8, 128), F32),
            pltpu.SemaphoreType.DMA((2, 2, 2)),
            pltpu.SemaphoreType.DMA((6,)),
            pltpu.SemaphoreType.REGULAR,
            pltpu.SemaphoreType.DMA((2, 2)),
            pltpu.SemaphoreType.DMA((6, 2)),
            pltpu.SemaphoreType.DMA((6, 3, 2)),
            pltpu.SemaphoreType.DMA((6, 2)),
            pltpu.SemaphoreType.DMA((2, 2)),
            pltpu.SemaphoreType.DMA((4,)),
        ],
        compiler_params=pltpu.CompilerParams(
            collective_id=0, has_side_effects=True, vmem_limit_bytes=40 << 20
        ),
    )(*(pltpu.with_memory_space_constraint(v, pltpu.HBM) for v in (tod, gap_mask, coupling.T, *(v.reshape(1, -1) for v in (taps, cross_det, cross_start, cross_src, src_owner)))))

    return pl.pallas_call(
        hand_out,
        out_shape=shapes,
        in_specs=[vmem] * 2,
        out_specs=(hbm, hbm),
        scratch_shapes=[pltpu.SemaphoreType.DMA((2,))],
        compiler_params=pltpu.CompilerParams(vmem_limit_bytes=1 << 20),
    )(*results)


def solution(mesh):
    return jax.shard_map(
        on_device,
        mesh=mesh,
        in_specs=(
            P(("wafer", "det"), None),
            P(("wafer", "det"), None),
            P(("wafer", "det"), None),
            P(),
            P(("wafer", "det")),
            P(("wafer", "det")),
            P(("wafer", "det")),
            P(),
        ),
        out_specs=(P(("wafer", "det"), None), P("wafer", "det", None)),
        check_vma=False,
    )
```

```python
import functools

import jax
import jax.numpy as jnp
from jax import lax
from jax.experimental import pallas as pl
from jax.experimental.pallas import tpu as pltpu
from jax.sharding import PartitionSpec as P

MESH = pl.DeviceIdType.MESH
F32 = jnp.float32
BF16 = jnp.bfloat16

ROWS = 64
NS = 8192
HALF = NS // 2
MODES = 32
TAPS = 129
CROSS = 64
RING = 4
DET = 32
SETS = (
    (0, 256, ("x", "y", "z")),
    (1024, 128, ("y", "z", "x")),
    (1536, 128, ("z", "x", "y")),
    (2048, 128, ("x", "y", "z")),
    (2560, 256, ("y", "z", "x")),
    (3584, 128, ("z", "x", "y")),
)
GROUPS = ((0, 1, 2), (3, 4, 5))
WIDE = HALF // len(GROUPS)
CHUNK = 512
PLACE = (0, 256, 384, 512, 640, 896)
BLOCKS = 1024


def split(v):
    hi = v.astype(BF16)
    lo = (v - hi.astype(F32)).astype(BF16)
    return hi, lo


def dot(a, b):
    return jnp.dot(a, b, preferred_element_type=F32)


def kernel(
    tod_hbm, mask_hbm, coup_hbm, taps_hbm, cdet_hbm, cstart_hbm, csrc_hbm, owner_hbm,
    filled, templ_ref,
    coup_ref, taps_ref, cdet_ref, cstart_ref, csrc_ref, owner_ref,
    tod, mask, model, res_hi, res_lo,
    part, acc, got_c, got_p, acc2, got3, amp,
    lhs_p, lhs_m, band,
    slots, dets, first_tile, shift, tod_snip, good_snip, snip, cnt, cnt_got, tsum, tsum_got,
    in_sem, small_sem, ready_sem, c_sem, p_sem, r_sem, g_sem, gc_sem, t_sem,
):
    wafer = lax.axis_index("wafer")
    det = lax.axis_index("det")
    core = lax.rem(det, 2)
    x = lax.rem(lax.div(det, 2), RING)
    y = lax.div(det, 2 * RING)
    coord = {"x": x, "y": y, "z": wafer}

    def reach(steps):
        at = {a: lax.rem(coord[a] + steps[a], RING) if steps.get(a) else coord[a] for a in coord}
        return (at["z"], (at["y"] * RING + at["x"]) * 2 + core)

    partner = (wafer, det + 1 - 2 * core)

    def remote(src, dst, send, recv, to):
        return pltpu.make_async_remote_copy(
            src_ref=src, dst_ref=dst, send_sem=send, recv_sem=recv,
            device_id=to, device_id_type=MESH,
        )

    def cols(first, width):
        return pl.ds(pl.multiple_of(first, 128), width)

    small = []
    for k, (src, dst) in enumerate((
        (coup_hbm, coup_ref), (taps_hbm, taps_ref), (cdet_hbm, cdet_ref),
        (cstart_hbm, cstart_ref), (csrc_hbm, csrc_ref), (owner_hbm, owner_ref),
    )):
        small.append(pltpu.make_async_copy(src, dst, small_sem.at[k]))
        small[-1].start()

    halves = (1 - core, core)
    loads = {}
    for g in range(len(GROUPS)):
        for h in range(2):
            span = cols(halves[h] * HALF + g * WIDE, WIDE)
            loads[h, g] = (
                pltpu.make_async_copy(tod_hbm.at[:, span], tod.at[:, span], in_sem.at[h, g, 0]),
                pltpu.make_async_copy(mask_hbm.at[:, span], mask.at[:, span], in_sem.at[h, g, 1]),
            )
            for one in loads[h, g]:
                one.start()

    lines = [reach({a: step}) for a in ("x", "y", "z") for step in range(1, RING)]
    barrier = pltpu.get_barrier_semaphore()
    for to in [partner] + lines:
        pl.semaphore_signal(barrier, inc=1, device_id=to, device_id_type=MESH)

    small[0].wait()
    coup_t = coup_ref[...]
    t_hi, t_lo = split(coup_t)
    w_hi, w_lo = split(coup_t * coup_t)
    zero = jnp.zeros((MODES, ROWS), BF16)
    lhs_p[0:32, :] = jnp.concatenate([t_hi, t_lo, t_hi, zero], axis=1)
    lhs_p[32:64, :] = jnp.concatenate([zero, zero, zero, w_hi], axis=1)
    lhs_p[64:96, :] = jnp.concatenate([zero, zero, zero, w_lo], axis=1)

    def partial_sums(first, width):
        span = cols(first, width)
        m = mask[:, span]
        v = jnp.where(m != 0, tod[:, span], 0.0)
        v_hi, v_lo = split(v)
        g = m.astype(F32).astype(BF16)
        out = dot(lhs_p[...], jnp.concatenate([v_hi, v_hi, v_lo, g], axis=0))
        return out[0:32], out[32:64] + out[64:96]

    def fill(h, g, dst):
        for one in loads[h, g]:
            one.wait()

        def body(i, carry):
            local = g * WIDE + i * CHUNK
            sums, weights = partial_sums(halves[h] * HALF + local, CHUNK)
            span = cols(local, CHUNK)
            for j in range(RING):
                dst[j, 0:8, span] = sums[8 * j:8 * j + 8]
                dst[j, 8:16, span] = weights[8 * j:8 * j + 8]
            return carry

        lax.fori_loop(0, WIDE // CHUNK, body, 0, unroll=True)

    copies_c = []
    for g in range(len(GROUPS)):
        span = pl.ds(g * WIDE, WIDE)
        copies_c.append(
            remote(part.at[:, :, span], got_c.at[:, :, span], c_sem.at[g, 0], c_sem.at[g, 1], partner)
        )
    fill(0, 0, part)
    pl.semaphore_wait(barrier, 1 + len(lines))
    copies_c[0].start()
    for to in lines:
        pl.semaphore_signal(ready_sem, inc=1, device_id=to, device_id_type=MESH)
    fill(1, 0, acc)
    fill(0, 1, part)
    copies_c[1].start()

    steps = sorted(
        ((p, q) for p in range(RING) for q in range(RING) if p or q),
        key=lambda v: -(min(v[0], RING - v[0]) + min(v[1], RING - v[1])),
    )
    on_line = [v for v in steps if not (v[0] and v[1])]
    off_line = [v for v in steps if v[0] and v[1]]

    def scatter(s, which):
        base, width, order = SETS[s]
        for p, q in which:
            block = cols(base + lax.rem(coord[order[0]] + p, RING) * width, width)
            remote(
                acc.at[lax.rem(coord[order[1]] + q, RING), :, block],
                got_p.at[steps.index((p, q)), :, pl.ds(PLACE[s], width)],
                p_sem.at[s, 0], p_sem.at[s, 1], reach({order[0]: p, order[1]: q}),
            ).start()

    def take(g):
        copies_c[g].wait_recv()
        span = pl.ds(g * WIDE, WIDE)
        acc[:, :, span] += got_c[:, :, span]

    take(0)
    for s in GROUPS[0]:
        scatter(s, on_line)
    fill(1, 1, acc)
    pl.semaphore_wait(ready_sem, len(lines))
    for s in GROUPS[0]:
        scatter(s, off_line)
    take(1)
    for s in GROUPS[1]:
        scatter(s, steps)

    for one in small[2:]:
        one.wait()
    owner = 2 * owner_ref[...]
    src_iota = lax.broadcasted_iota(jnp.int32, (128, CROSS), 0)
    of_src = (src_iota == csrc_ref[...]).astype(F32).astype(BF16)
    row_iota = lax.broadcasted_iota(jnp.int32, (256, 128), 0)
    perm0 = (row_iota == owner).astype(F32).astype(BF16)
    perm1 = (row_iota == owner + 1).astype(F32).astype(BF16)
    oh_t = jnp.concatenate([dot(perm0, of_src), dot(perm1, of_src)], axis=1)
    slots[:, 0:128] = oh_t.astype(BF16)
    slots[:, 128:256] = oh_t.astype(BF16)
    det_iota = lax.broadcasted_iota(jnp.int32, (ROWS, CROSS), 0)
    of_det = (det_iota == cdet_ref[...]).astype(F32).T.astype(BF16)
    dets[...] = jnp.concatenate([of_det, of_det], axis=1)
    start = jnp.broadcast_to(cstart_ref[...], (128, CROSS)).T
    first_tile[...] = start >> 7
    shift[...] = start & 127
    c_hi, c_lo = split(coup_ref[...].T)
    lhs_m[0:ROWS, :] = jnp.concatenate([c_hi, c_lo, c_hi], axis=1)
    lhs_m[ROWS:ROWS + CROSS, :] = dot(of_det, lhs_m[0:ROWS, :]).astype(BF16)
    cnt[...] = jnp.broadcast_to(jnp.sum(oh_t, axis=1, keepdims=True), (256, 128)).reshape(DET, 8, 128)

    small[1].wait()
    line = jnp.concatenate([taps_ref[...], jnp.zeros((1, 256 - TAPS), F32)], axis=1)
    turned = pltpu.roll(jnp.broadcast_to(line, (128, 256)), 192, 1, stride=1, stride_axis=0)
    b_hi, b_lo = split(turned.T)
    band[:, 0:128] = b_hi
    band[:, 128:256] = b_lo

    def choose(b, lines, wide):
        tile = first_tile[...]
        at = {v: tile == b * 4 + v for v in range(-2, 4)}
        wide = list(wide)
        for q in range(4):
            for w in range(3):
                for k, line in enumerate(lines):
                    wide[3 * k + w] = jnp.where(at[q - w], line[:, 128 * q:128 * q + 128], wide[3 * k + w])
        return tuple(wide)

    def shifted(wide):
        rows = jnp.concatenate(wide, axis=1)
        rest = jnp.concatenate([shift[...]] * 3, axis=1)
        for bit in range(7):
            moved = pltpu.roll(rows, 384 - (1 << bit), 1)
            rows = jnp.where((rest & (1 << bit)) != 0, moved, rows)
        return rows[:, 0:256]

    no_tiles = (jnp.zeros((CROSS, 128), F32),) * 3

    def input_block(b, wide):
        span = cols(b * 512, 512)
        m = mask[:, span]
        v_hi, v_lo = split(jnp.where(m != 0, tod[:, span], 0.0))
        g = m.astype(F32).astype(BF16)
        lines = dot(dets[...], jnp.concatenate([v_hi, v_lo], axis=0)), dot(dets[:, 0:ROWS], g)
        return choose(b, lines, wide)

    inputs = lax.fori_loop(0, NS // 512, input_block, no_tiles * 2)
    tod_snip[...] = shifted(inputs[0:3])
    good_snip[...] = shifted(inputs[3:6])
    for edge in (res_hi, res_lo):
        edge[:, 0:128] = jnp.zeros((ROWS, 128), BF16)
        edge[:, 128 + NS:256 + NS] = jnp.zeros((ROWS, 128), BF16)

    def from_plane(s, rows, sems):
        every = got_p.at[:, 0:rows, pl.ds(PLACE[s], SETS[s][1])]
        return remote(every, every, sems.at[s, 0], sems.at[s, 1], partner)

    axis3 = []
    for s, (base, width, order) in enumerate(SETS):
        from_plane(s, 16, p_sem).wait_recv()
        span = pl.ds(PLACE[s], width)
        total = acc[coord[order[1]], :, cols(base + coord[order[0]] * width, width)]
        for k in range(len(steps)):
            total += got_p[k, :, span]
        acc2[:, span] = total
        for step in range(1, RING):
            axis3.append(remote(
                acc2.at[:, span], got3.at[step - 1, :, span],
                r_sem.at[s, step - 1, 0], r_sem.at[s, step - 1, 1], reach({order[2]: step}),
            ))
            axis3[-1].start()

    for s, (base, width, order) in enumerate(SETS):
        for one in axis3[3 * s:3 * s + 3]:
            one.wait_recv()
        span = pl.ds(PLACE[s], width)
        whole = (acc2[:, span] + got3[0, :, span]) + (got3[1, :, span] + got3[2, :, span])
        block = cols(core * HALF + base + coord[order[0]] * width, width)
        amp[coord[order[1]], :, block] = whole[0:8] / (whole[8:16] + 1.0)
        here = amp.at[coord[order[1]], :, block]
        for p, q in steps:
            remote(here, here, g_sem.at[s, 0], g_sem.at[s, 1], reach({order[0]: p, order[1]: q})).start()

    owners = []
    for p, q in steps + [(0, 0)]:
        for other in (0, 1):
            if p or q or other:
                at = reach({"x": p, "y": q})[1]
                owners.append(at + other * (1 - 2 * core))

    def to_owners(src, dst, send, recv):
        for k, to in enumerate(owners):
            remote(src.at[to], dst.at[k], send, recv, (wafer, to)).start()

    def model_block(b, wide):
        span = cols(b * 512, 512)
        a_hi, a_lo = split(amp[:, :, span].reshape(MODES, 512))
        value = dot(lhs_m[...], jnp.concatenate([a_hi, a_hi, a_lo], axis=0))
        model[:, span] = value[0:ROWS]
        return choose(b, (value[ROWS:ROWS + CROSS],), wide)

    def resid_blocks(side, g):
        for b in range(WIDE // CHUNK):
            first = side * HALF + g * WIDE + b * CHUNK
            span = cols(first, CHUNK)
            r_hi, r_lo = split(jnp.where(mask[:, span] != 0, tod[:, span] - model[:, span], 0.0))
            res_hi[:, cols(first + 128, CHUNK)] = r_hi
            res_lo[:, cols(first + 128, CHUNK)] = r_lo

    def model_blocks(side, g, wide):
        for b in range(WIDE // CHUNK):
            wide = model_block((side * HALF + g * WIDE) // CHUNK + b, wide)
        return wide

    wide = no_tiles
    copies_a = []
    for g, members in enumerate(GROUPS):
        for s in members:
            from_plane(s, 8, g_sem).wait_recv()
        half = amp.at[:, :, cols(core * HALF + g * WIDE, WIDE)]
        copies_a.append(remote(half, half, gc_sem.at[g, 0], gc_sem.at[g, 1], partner))
        copies_a[g].start()
        wide = model_blocks(core, g, wide)
        if g == 0:
            to_owners(cnt, cnt_got, t_sem.at[0], t_sem.at[1])
        resid_blocks(core, g)
        if g > 0:
            resid_blocks(1 - core, g - 1)
        copies_a[g].wait_recv()
        wide = model_blocks(1 - core, g, wide)

    rows = jnp.where(good_snip[...] != 0.0, tod_snip[...] - shifted(wide), 0.0)
    snip[0:CROSS, :] = rows[:, 0:128]
    snip[CROSS:2 * CROSS, :] = rows[:, 128:256]
    s_hi, s_lo = split(snip[...])
    tsum[...] = dot(slots[...], jnp.concatenate([s_hi, s_lo], axis=0)).reshape(DET, 8, 128)
    to_owners(tsum, tsum_got, t_sem.at[2], t_sem.at[3])

    resid_blocks(1 - core, len(GROUPS) - 1)
    lane64 = lax.broadcasted_iota(jnp.int32, (ROWS, 128), 1) < 64

    def fill_block(b, carry):
        pieces = []
        for res in (res_hi, res_lo):
            left = []
            for q in range(4):
                before = res[:, cols(b * 512 + q * 128, 128)]
                here = res[:, cols(b * 512 + q * 128 + 128, 128)]
                after = res[:, cols(b * 512 + q * 128 + 256, 128)]
                left.append(jnp.concatenate([here, jnp.where(lane64, after, before)], axis=1))
            pieces.append(jnp.concatenate(left, axis=0))
        l_hi, l_lo = pieces
        first = dot(l_hi, band[...])
        second = dot(l_lo, band[:, 0:128])
        smooth = first[:, 0:128] + (first[:, 128:256] + second)
        for q in range(4):
            span = cols(b * 512 + q * 128, 128)
            filled[:, span] = jnp.where(
                mask[:, span] != 0, tod[:, span], model[:, span] + smooth[q * ROWS:(q + 1) * ROWS]
            )
        return carry

    lax.fori_loop(0, NS // 512, fill_block, 0)

    def wait_all(src, dst, send, recv):
        every = remote(src.at[0:DET - 1], dst.at[0:DET - 1], send, recv, partner)
        every.wait_recv()
        every.wait_send()

    for one in copies_c + copies_a + axis3:
        one.wait_send()
    for s in range(len(SETS)):
        from_plane(s, 16, p_sem).wait_send()
        from_plane(s, 8, g_sem).wait_send()

    wait_all(cnt, cnt_got, t_sem.at[0], t_sem.at[1])
    number = cnt[det]
    for k in range(DET - 1):
        number += cnt_got[k]
    wait_all(tsum, tsum_got, t_sem.at[2], t_sem.at[3])
    total = tsum[det]
    for k in range(DET - 1):
        total += tsum_got[k]
    snip[0:8, :] = total / (number + 1.0)
    for o in range(4):
        templ_ref[0, o:o + 1, 0:128] = snip[2 * o:2 * o + 1, :]
        templ_ref[0, o:o + 1, 128:256] = snip[2 * o + 1:2 * o + 2, :]


def hand_out(filled, templ, filled_out, templ_out, sem):
    copies = [pltpu.make_async_copy(templ, templ_out, sem.at[8])]
    for k in range(8):
        strip = pl.ds(8 * k, 8)
        copies.append(pltpu.make_async_copy(filled.at[strip], filled_out.at[strip], sem.at[k]))
    for one in copies:
        one.start()
    for one in copies:
        one.wait()


def on_device(tod, gap_mask, coupling, taps, cross_det, cross_start, cross_src, src_owner):
    vmem, hbm = (pl.BlockSpec(memory_space=m) for m in (pltpu.VMEM, pltpu.HBM))
    shapes = (jax.ShapeDtypeStruct((ROWS, NS), F32), jax.ShapeDtypeStruct((1, 4, 256), F32))
    results = pl.pallas_call(
        kernel,
        out_shape=shapes,
        in_specs=[hbm] * 8,
        out_specs=(vmem, vmem),
        scratch_shapes=[
            pltpu.VMEM((MODES, ROWS), F32),
            pltpu.VMEM((1, TAPS), F32),
            pltpu.VMEM((1, CROSS), jnp.int32),
            pltpu.VMEM((1, CROSS), jnp.int32),
            pltpu.VMEM((1, CROSS), jnp.int32),
            pltpu.VMEM((1, 128), jnp.int32),
            pltpu.VMEM((ROWS, NS), F32),
            pltpu.VMEM((ROWS, NS), jnp.int32),
            pltpu.VMEM((ROWS, NS), F32),
            pltpu.VMEM((ROWS, NS + 256), BF16),
            pltpu.VMEM((ROWS, NS + 256), BF16),
            pltpu.VMEM((RING, 16, HALF), F32),
            pltpu.VMEM((RING, 16, HALF), F32),
            pltpu.VMEM((RING, 16, HALF), F32),
            pltpu.VMEM((RING * RING - 1, 16, BLOCKS), F32),
            pltpu.VMEM((16, BLOCKS), F32),
            pltpu.VMEM((3, 16, BLOCKS), F32),
            pltpu.VMEM((RING, 8, NS), F32),
            pltpu.VMEM((96, 256), BF16),
            pltpu.VMEM((ROWS + CROSS, 96), BF16),
            pltpu.VMEM((256, 256), BF16),
            pltpu.VMEM((256, 256), BF16),
            pltpu.VMEM((CROSS, 128), BF16),
            pltpu.VMEM((CROSS, 128), jnp.int32),
            pltpu.VMEM((CROSS, 128), jnp.int32),
            pltpu.VMEM((CROSS, 256), F32),
            pltpu.VMEM((CROSS, 256), F32),
            pltpu.VMEM((2 * CROSS, 128), F32),
            pltpu.VMEM((DET, 8, 128), F32),
            pltpu.VMEM((DET, 8, 128), F32),
            pltpu.VMEM((DET, 8, 128), F32),
            pltpu.VMEM((DET, 8, 128), F32),
            pltpu.SemaphoreType.DMA((2, 2, 2)),
            pltpu.SemaphoreType.DMA((6,)),
            pltpu.SemaphoreType.REGULAR,
            pltpu.SemaphoreType.DMA((2, 2)),
            pltpu.SemaphoreType.DMA((6, 2)),
            pltpu.SemaphoreType.DMA((6, 3, 2)),
            pltpu.SemaphoreType.DMA((6, 2)),
            pltpu.SemaphoreType.DMA((2, 2)),
            pltpu.SemaphoreType.DMA((4,)),
        ],
        compiler_params=pltpu.CompilerParams(
            collective_id=0, has_side_effects=True, vmem_limit_bytes=40 << 20
        ),
    )(*(pltpu.with_memory_space_constraint(v, pltpu.HBM) for v in (tod, gap_mask, coupling.T, *(v.reshape(1, -1) for v in (taps, cross_det, cross_start, cross_src, src_owner)))))

    return pl.pallas_call(
        hand_out,
        out_shape=shapes,
        in_specs=[vmem] * 2,
        out_specs=(hbm, hbm),
        scratch_shapes=[pltpu.SemaphoreType.DMA((9,))],
        compiler_params=pltpu.CompilerParams(vmem_limit_bytes=1 << 20),
    )(*results)


def solution(mesh):
    return jax.shard_map(
        on_device,
        mesh=mesh,
        in_specs=(
            P(("wafer", "det"), None),
            P(("wafer", "det"), None),
            P(("wafer", "det"), None),
            P(),
            P(("wafer", "det")),
            P(("wafer", "det")),
            P(("wafer", "det")),
            P(),
        ),
        out_specs=(P(("wafer", "det"), None), P("wafer", "det", None)),
        check_vma=False,
    )
```

```python
import functools

import jax
import jax.numpy as jnp
from jax import lax
from jax.experimental import pallas as pl
from jax.experimental.pallas import tpu as pltpu
from jax.sharding import PartitionSpec as P

MESH = pl.DeviceIdType.MESH
F32 = jnp.float32
BF16 = jnp.bfloat16

ROWS = 64
NS = 8192
HALF = NS // 2
MODES = 32
TAPS = 129
CROSS = 64
RING = 4
DET = 32
SETS = (
    (0, 256, ("x", "y", "z")),
    (1024, 128, ("y", "z", "x")),
    (1536, 128, ("z", "x", "y")),
    (2048, 128, ("x", "y", "z")),
    (2560, 256, ("y", "z", "x")),
    (3584, 128, ("z", "x", "y")),
)
GROUPS = ((0, 1, 2), (3, 4, 5))
WIDE = HALF // len(GROUPS)
CHUNK = 512
PLACE = (0, 256, 384, 512, 640, 896)
BLOCKS = 1024


def split(v):
    hi = v.astype(BF16)
    lo = (v - hi.astype(F32)).astype(BF16)
    return hi, lo


def dot(a, b):
    return jnp.dot(a, b, preferred_element_type=F32)


def kernel(
    tod_hbm, mask_hbm, coup_hbm, taps_hbm, cdet_hbm, cstart_hbm, csrc_hbm, owner_hbm,
    filled, templ_ref,
    coup_ref, taps_ref, cdet_ref, cstart_ref, csrc_ref, owner_ref,
    tod, mask, model, res_hi, res_lo,
    part, acc, got_c, got_p, acc2, got3, amp,
    lhs_p, lhs_m, band,
    slots, dets, first_tile, shift, tod_snip, good_snip, snip, cnt, cnt_got, tsum, tsum_got,
    in_sem, small_sem, ready_sem, c_sem, p_sem, r_sem, g_sem, gc_sem, t_sem,
):
    wafer = lax.axis_index("wafer")
    det = lax.axis_index("det")
    core = lax.rem(det, 2)
    x = lax.rem(lax.div(det, 2), RING)
    y = lax.div(det, 2 * RING)
    coord = {"x": x, "y": y, "z": wafer}

    def reach(steps):
        at = {a: lax.rem(coord[a] + steps[a], RING) if steps.get(a) else coord[a] for a in coord}
        return (at["z"], (at["y"] * RING + at["x"]) * 2 + core)

    partner = (wafer, det + 1 - 2 * core)

    def remote(src, dst, send, recv, to):
        return pltpu.make_async_remote_copy(
            src_ref=src, dst_ref=dst, send_sem=send, recv_sem=recv,
            device_id=to, device_id_type=MESH,
        )

    def cols(first, width):
        return pl.ds(pl.multiple_of(first, 128), width)

    small = []
    for k, (src, dst) in enumerate((
        (coup_hbm, coup_ref), (taps_hbm, taps_ref), (cdet_hbm, cdet_ref),
        (cstart_hbm, cstart_ref), (csrc_hbm, csrc_ref), (owner_hbm, owner_ref),
    )):
        small.append(pltpu.make_async_copy(src, dst, small_sem.at[k]))
        small[-1].start()

    halves = (1 - core, core)
    loads = {}
    for g in range(len(GROUPS)):
        for h in range(2):
            span = cols(halves[h] * HALF + g * WIDE, WIDE)
            loads[h, g] = (
                pltpu.make_async_copy(tod_hbm.at[:, span], tod.at[:, span], in_sem.at[h, g, 0]),
                pltpu.make_async_copy(mask_hbm.at[:, span], mask.at[:, span], in_sem.at[h, g, 1]),
            )
            for one in loads[h, g]:
                one.start()

    lines = [reach({a: step}) for a in ("x", "y", "z") for step in range(1, RING)]
    barrier = pltpu.get_barrier_semaphore()
    for to in [partner] + lines:
        pl.semaphore_signal(barrier, inc=1, device_id=to, device_id_type=MESH)

    small[0].wait()
    coup_t = coup_ref[...]
    t_hi, t_lo = split(coup_t)
    w_hi, w_lo = split(coup_t * coup_t)
    zero = jnp.zeros((MODES, ROWS), BF16)
    lhs_p[0:32, :] = jnp.concatenate([t_hi, t_lo, t_hi, zero], axis=1)
    lhs_p[32:64, :] = jnp.concatenate([zero, zero, zero, w_hi], axis=1)
    lhs_p[64:96, :] = jnp.concatenate([zero, zero, zero, w_lo], axis=1)

    def partial_sums(first, width):
        span = cols(first, width)
        m = mask[:, span]
        v = jnp.where(m != 0, tod[:, span], 0.0)
        v_hi, v_lo = split(v)
        g = m.astype(F32).astype(BF16)
        out = dot(lhs_p[...], jnp.concatenate([v_hi, v_hi, v_lo, g], axis=0))
        return out[0:32], out[32:64] + out[64:96]

    def fill(h, g, dst):
        for one in loads[h, g]:
            one.wait()

        def body(i, carry):
            local = g * WIDE + i * CHUNK
            sums, weights = partial_sums(halves[h] * HALF + local, CHUNK)
            span = cols(local, CHUNK)
            for j in range(RING):
                dst[j, 0:8, span] = sums[8 * j:8 * j + 8]
                dst[j, 8:16, span] = weights[8 * j:8 * j + 8]
            return carry

        lax.fori_loop(0, WIDE // CHUNK, body, 0, unroll=True)

    copies_c = []
    for g in range(len(GROUPS)):
        span = pl.ds(g * WIDE, WIDE)
        copies_c.append(
            remote(part.at[:, :, span], got_c.at[:, :, span], c_sem.at[g, 0], c_sem.at[g, 1], partner)
        )
    fill(0, 0, part)
    pl.semaphore_wait(barrier, 1 + len(lines))
    copies_c[0].start()
    for to in lines:
        pl.semaphore_signal(ready_sem, inc=1, device_id=to, device_id_type=MESH)
    fill(1, 0, acc)
    fill(0, 1, part)
    copies_c[1].start()

    steps = sorted(
        ((p, q) for p in range(RING) for q in range(RING) if p or q),
        key=lambda v: -(min(v[0], RING - v[0]) + min(v[1], RING - v[1])),
    )
    on_line = [v for v in steps if not (v[0] and v[1])]
    off_line = [v for v in steps if v[0] and v[1]]

    def scatter(s, which):
        base, width, order = SETS[s]
        for p, q in which:
            block = cols(base + lax.rem(coord[order[0]] + p, RING) * width, width)
            remote(
                acc.at[lax.rem(coord[order[1]] + q, RING), :, block],
                got_p.at[steps.index((p, q)), :, pl.ds(PLACE[s], width)],
                p_sem.at[s, 0], p_sem.at[s, 1], reach({order[0]: p, order[1]: q}),
            ).start()

    def take(g):
        copies_c[g].wait_recv()
        span = pl.ds(g * WIDE, WIDE)
        acc[:, :, span] += got_c[:, :, span]

    take(0)
    for v in on_line:
        for s in GROUPS[0]:
            scatter(s, [v])
    fill(1, 1, acc)
    pl.semaphore_wait(ready_sem, len(lines))
    for v in off_line:
        for s in GROUPS[0]:
            scatter(s, [v])
    take(1)
    for v in steps:
        for s in GROUPS[1]:
            scatter(s, [v])

    for one in small[2:]:
        one.wait()
    owner = 2 * owner_ref[...]
    src_iota = lax.broadcasted_iota(jnp.int32, (128, CROSS), 0)
    of_src = (src_iota == csrc_ref[...]).astype(F32).astype(BF16)
    row_iota = lax.broadcasted_iota(jnp.int32, (256, 128), 0)
    perm0 = (row_iota == owner).astype(F32).astype(BF16)
    perm1 = (row_iota == owner + 1).astype(F32).astype(BF16)
    oh_t = jnp.concatenate([dot(perm0, of_src), dot(perm1, of_src)], axis=1)
    slots[:, 0:128] = oh_t.astype(BF16)
    slots[:, 128:256] = oh_t.astype(BF16)
    det_iota = lax.broadcasted_iota(jnp.int32, (ROWS, CROSS), 0)
    of_det = (det_iota == cdet_ref[...]).astype(F32).T.astype(BF16)
    dets[...] = jnp.concatenate([of_det, of_det], axis=1)
    start = jnp.broadcast_to(cstart_ref[...], (128, CROSS)).T
    first_tile[...] = start >> 7
    shift[...] = start & 127
    c_hi, c_lo = split(coup_ref[...].T)
    lhs_m[0:ROWS, :] = jnp.concatenate([c_hi, c_lo, c_hi], axis=1)
    lhs_m[ROWS:ROWS + CROSS, :] = dot(of_det, lhs_m[0:ROWS, :]).astype(BF16)
    cnt[...] = jnp.broadcast_to(jnp.sum(oh_t, axis=1, keepdims=True), (256, 128)).reshape(DET, 8, 128)

    small[1].wait()
    line = jnp.concatenate([taps_ref[...], jnp.zeros((1, 256 - TAPS), F32)], axis=1)
    turned = pltpu.roll(jnp.broadcast_to(line, (128, 256)), 192, 1, stride=1, stride_axis=0)
    b_hi, b_lo = split(turned.T)
    band[:, 0:128] = b_hi
    band[:, 128:256] = b_lo

    def choose(b, lines, wide):
        tile = first_tile[...]
        at = {v: tile == b * 4 + v for v in range(-2, 4)}
        wide = list(wide)
        for q in range(4):
            for w in range(3):
                for k, line in enumerate(lines):
                    wide[3 * k + w] = jnp.where(at[q - w], line[:, 128 * q:128 * q + 128], wide[3 * k + w])
        return tuple(wide)

    def shifted(wide):
        rows = jnp.concatenate(wide, axis=1)
        rest = jnp.concatenate([shift[...]] * 3, axis=1)
        for bit in range(7):
            moved = pltpu.roll(rows, 384 - (1 << bit), 1)
            rows = jnp.where((rest & (1 << bit)) != 0, moved, rows)
        return rows[:, 0:256]

    no_tiles = (jnp.zeros((CROSS, 128), F32),) * 3

    def input_block(b, wide):
        span = cols(b * 512, 512)
        m = mask[:, span]
        v_hi, v_lo = split(jnp.where(m != 0, tod[:, span], 0.0))
        g = m.astype(F32).astype(BF16)
        lines = dot(dets[...], jnp.concatenate([v_hi, v_lo], axis=0)), dot(dets[:, 0:ROWS], g)
        return choose(b, lines, wide)

    inputs = lax.fori_loop(0, NS // 512, input_block, no_tiles * 2)
    tod_snip[...] = shifted(inputs[0:3])
    good_snip[...] = shifted(inputs[3:6])
    for edge in (res_hi, res_lo):
        edge[:, 0:128] = jnp.zeros((ROWS, 128), BF16)
        edge[:, 128 + NS:256 + NS] = jnp.zeros((ROWS, 128), BF16)

    def from_plane(s, rows, sems):
        every = got_p.at[:, 0:rows, pl.ds(PLACE[s], SETS[s][1])]
        return remote(every, every, sems.at[s, 0], sems.at[s, 1], partner)

    axis3 = []
    for s, (base, width, order) in enumerate(SETS):
        from_plane(s, 16, p_sem).wait_recv()
        span = pl.ds(PLACE[s], width)
        total = acc[coord[order[1]], :, cols(base + coord[order[0]] * width, width)]
        for k in range(len(steps)):
            total += got_p[k, :, span]
        acc2[:, span] = total
        for step in range(1, RING):
            axis3.append(remote(
                acc2.at[:, span], got3.at[step - 1, :, span],
                r_sem.at[s, step - 1, 0], r_sem.at[s, step - 1, 1], reach({order[2]: step}),
            ))
            axis3[-1].start()

    for s, (base, width, order) in enumerate(SETS):
        for one in axis3[3 * s:3 * s + 3]:
            one.wait_recv()
        span = pl.ds(PLACE[s], width)
        whole = (acc2[:, span] + got3[0, :, span]) + (got3[1, :, span] + got3[2, :, span])
        block = cols(core * HALF + base + coord[order[0]] * width, width)
        amp[coord[order[1]], :, block] = whole[0:8] / (whole[8:16] + 1.0)
        here = amp.at[coord[order[1]], :, block]
        for p, q in steps:
            remote(here, here, g_sem.at[s, 0], g_sem.at[s, 1], reach({order[0]: p, order[1]: q})).start()

    owners = []
    for p, q in steps + [(0, 0)]:
        for other in (0, 1):
            if p or q or other:
                at = reach({"x": p, "y": q})[1]
                owners.append(at + other * (1 - 2 * core))

    def to_owners(src, dst, send, recv):
        for k, to in enumerate(owners):
            remote(src.at[to], dst.at[k], send, recv, (wafer, to)).start()

    def model_block(b, wide):
        span = cols(b * 512, 512)
        a_hi, a_lo = split(amp[:, :, span].reshape(MODES, 512))
        value = dot(lhs_m[...], jnp.concatenate([a_hi, a_hi, a_lo], axis=0))
        model[:, span] = value[0:ROWS]
        return choose(b, (value[ROWS:ROWS + CROSS],), wide)

    def resid_blocks(side, g):
        for b in range(WIDE // CHUNK):
            first = side * HALF + g * WIDE + b * CHUNK
            span = cols(first, CHUNK)
            r_hi, r_lo = split(jnp.where(mask[:, span] != 0, tod[:, span] - model[:, span], 0.0))
            res_hi[:, cols(first + 128, CHUNK)] = r_hi
            res_lo[:, cols(first + 128, CHUNK)] = r_lo

    def model_blocks(side, g, wide):
        for b in range(WIDE // CHUNK):
            wide = model_block((side * HALF + g * WIDE) // CHUNK + b, wide)
        return wide

    wide = no_tiles
    copies_a = []
    for g, members in enumerate(GROUPS):
        for s in members:
            from_plane(s, 8, g_sem).wait_recv()
        half = amp.at[:, :, cols(core * HALF + g * WIDE, WIDE)]
        copies_a.append(remote(half, half, gc_sem.at[g, 0], gc_sem.at[g, 1], partner))
        copies_a[g].start()
        wide = model_blocks(core, g, wide)
        if g == 0:
            to_owners(cnt, cnt_got, t_sem.at[0], t_sem.at[1])
        resid_blocks(core, g)
        if g > 0:
            resid_blocks(1 - core, g - 1)
        copies_a[g].wait_recv()
        wide = model_blocks(1 - core, g, wide)

    rows = jnp.where(good_snip[...] != 0.0, tod_snip[...] - shifted(wide), 0.0)
    snip[0:CROSS, :] = rows[:, 0:128]
    snip[CROSS:2 * CROSS, :] = rows[:, 128:256]
    s_hi, s_lo = split(snip[...])
    tsum[...] = dot(slots[...], jnp.concatenate([s_hi, s_lo], axis=0)).reshape(DET, 8, 128)
    to_owners(tsum, tsum_got, t_sem.at[2], t_sem.at[3])

    resid_blocks(1 - core, len(GROUPS) - 1)
    lane64 = lax.broadcasted_iota(jnp.int32, (ROWS, 128), 1) < 64

    def fill_block(b, carry):
        pieces = []
        for res in (res_hi, res_lo):
            left = []
            for q in range(4):
                before = res[:, cols(b * 512 + q * 128, 128)]
                here = res[:, cols(b * 512 + q * 128 + 128, 128)]
                after = res[:, cols(b * 512 + q * 128 + 256, 128)]
                left.append(jnp.concatenate([here, jnp.where(lane64, after, before)], axis=1))
            pieces.append(jnp.concatenate(left, axis=0))
        l_hi, l_lo = pieces
        first = dot(l_hi, band[...])
        second = dot(l_lo, band[:, 0:128])
        smooth = first[:, 0:128] + (first[:, 128:256] + second)
        for q in range(4):
            span = cols(b * 512 + q * 128, 128)
            filled[:, span] = jnp.where(
                mask[:, span] != 0, tod[:, span], model[:, span] + smooth[q * ROWS:(q + 1) * ROWS]
            )
        return carry

    lax.fori_loop(0, NS // 512, fill_block, 0)

    def wait_all(src, dst, send, recv):
        every = remote(src.at[0:DET - 1], dst.at[0:DET - 1], send, recv, partner)
        every.wait_recv()
        every.wait_send()

    for one in copies_c + copies_a + axis3:
        one.wait_send()
    for s in range(len(SETS)):
        from_plane(s, 16, p_sem).wait_send()
        from_plane(s, 8, g_sem).wait_send()

    wait_all(cnt, cnt_got, t_sem.at[0], t_sem.at[1])
    number = cnt[det]
    for k in range(DET - 1):
        number += cnt_got[k]
    wait_all(tsum, tsum_got, t_sem.at[2], t_sem.at[3])
    total = tsum[det]
    for k in range(DET - 1):
        total += tsum_got[k]
    snip[0:8, :] = total / (number + 1.0)
    for o in range(4):
        templ_ref[0, o:o + 1, 0:128] = snip[2 * o:2 * o + 1, :]
        templ_ref[0, o:o + 1, 128:256] = snip[2 * o + 1:2 * o + 2, :]


def hand_out(filled, templ, filled_out, templ_out, sem):
    copies = [pltpu.make_async_copy(templ, templ_out, sem.at[8])]
    for k in range(8):
        strip = pl.ds(8 * k, 8)
        copies.append(pltpu.make_async_copy(filled.at[strip], filled_out.at[strip], sem.at[k]))
    for one in copies:
        one.start()
    for one in copies:
        one.wait()


def on_device(tod, gap_mask, coupling, taps, cross_det, cross_start, cross_src, src_owner):
    vmem, hbm = (pl.BlockSpec(memory_space=m) for m in (pltpu.VMEM, pltpu.HBM))
    shapes = (jax.ShapeDtypeStruct((ROWS, NS), F32), jax.ShapeDtypeStruct((1, 4, 256), F32))
    results = pl.pallas_call(
        kernel,
        out_shape=shapes,
        in_specs=[hbm] * 8,
        out_specs=(vmem, vmem),
        scratch_shapes=[
            pltpu.VMEM((MODES, ROWS), F32),
            pltpu.VMEM((1, TAPS), F32),
            pltpu.VMEM((1, CROSS), jnp.int32),
            pltpu.VMEM((1, CROSS), jnp.int32),
            pltpu.VMEM((1, CROSS), jnp.int32),
            pltpu.VMEM((1, 128), jnp.int32),
            pltpu.VMEM((ROWS, NS), F32),
            pltpu.VMEM((ROWS, NS), jnp.int32),
            pltpu.VMEM((ROWS, NS), F32),
            pltpu.VMEM((ROWS, NS + 256), BF16),
            pltpu.VMEM((ROWS, NS + 256), BF16),
            pltpu.VMEM((RING, 16, HALF), F32),
            pltpu.VMEM((RING, 16, HALF), F32),
            pltpu.VMEM((RING, 16, HALF), F32),
            pltpu.VMEM((RING * RING - 1, 16, BLOCKS), F32),
            pltpu.VMEM((16, BLOCKS), F32),
            pltpu.VMEM((3, 16, BLOCKS), F32),
            pltpu.VMEM((RING, 8, NS), F32),
            pltpu.VMEM((96, 256), BF16),
            pltpu.VMEM((ROWS + CROSS, 96), BF16),
            pltpu.VMEM((256, 256), BF16),
            pltpu.VMEM((256, 256), BF16),
            pltpu.VMEM((CROSS, 128), BF16),
            pltpu.VMEM((CROSS, 128), jnp.int32),
            pltpu.VMEM((CROSS, 128), jnp.int32),
            pltpu.VMEM((CROSS, 256), F32),
            pltpu.VMEM((CROSS, 256), F32),
            pltpu.VMEM((2 * CROSS, 128), F32),
            pltpu.VMEM((DET, 8, 128), F32),
            pltpu.VMEM((DET, 8, 128), F32),
            pltpu.VMEM((DET, 8, 128), F32),
            pltpu.VMEM((DET, 8, 128), F32),
            pltpu.SemaphoreType.DMA((2, 2, 2)),
            pltpu.SemaphoreType.DMA((6,)),
            pltpu.SemaphoreType.REGULAR,
            pltpu.SemaphoreType.DMA((2, 2)),
            pltpu.SemaphoreType.DMA((6, 2)),
            pltpu.SemaphoreType.DMA((6, 3, 2)),
            pltpu.SemaphoreType.DMA((6, 2)),
            pltpu.SemaphoreType.DMA((2, 2)),
            pltpu.SemaphoreType.DMA((4,)),
        ],
        compiler_params=pltpu.CompilerParams(
            collective_id=0, has_side_effects=True, vmem_limit_bytes=40 << 20
        ),
    )(*(pltpu.with_memory_space_constraint(v, pltpu.HBM) for v in (tod, gap_mask, coupling.T, *(v.reshape(1, -1) for v in (taps, cross_det, cross_start, cross_src, src_owner)))))

    return pl.pallas_call(
        hand_out,
        out_shape=shapes,
        in_specs=[vmem] * 2,
        out_specs=(hbm, hbm),
        scratch_shapes=[pltpu.SemaphoreType.DMA((9,))],
        compiler_params=pltpu.CompilerParams(vmem_limit_bytes=1 << 20),
    )(*results)


def solution(mesh):
    return jax.shard_map(
        on_device,
        mesh=mesh,
        in_specs=(
            P(("wafer", "det"), None),
            P(("wafer", "det"), None),
            P(("wafer", "det"), None),
            P(),
            P(("wafer", "det")),
            P(("wafer", "det")),
            P(("wafer", "det")),
            P(),
        ),
        out_specs=(P(("wafer", "det"), None), P("wafer", "det", None)),
        check_vma=False,
    )
```

```python
import functools

import jax
import jax.numpy as jnp
from jax import lax
from jax.experimental import pallas as pl
from jax.experimental.pallas import tpu as pltpu
from jax.sharding import PartitionSpec as P

MESH = pl.DeviceIdType.MESH
F32 = jnp.float32
BF16 = jnp.bfloat16

ROWS = 64
NS = 8192
HALF = NS // 2
MODES = 32
TAPS = 129
CROSS = 64
RING = 4
DET = 32
SETS = (
    (0, 256, ("x", "y", "z")),
    (1024, 128, ("y", "z", "x")),
    (1536, 128, ("z", "x", "y")),
    (2048, 128, ("x", "y", "z")),
    (2560, 256, ("y", "z", "x")),
    (3584, 128, ("z", "x", "y")),
)
GROUPS = ((0, 1, 2), (3, 4, 5))
WIDE = HALF // len(GROUPS)
CHUNK = 512
PLACE = (0, 256, 384, 512, 640, 896)
BLOCKS = 1024


def split(v):
    hi = v.astype(BF16)
    lo = (v - hi.astype(F32)).astype(BF16)
    return hi, lo


def dot(a, b):
    return jnp.dot(a, b, preferred_element_type=F32)


def kernel(
    tod_hbm, mask_hbm, coup_hbm, taps_hbm, cdet_hbm, cstart_hbm, csrc_hbm, owner_hbm,
    filled, templ_ref,
    coup_ref, taps_ref, cdet_ref, cstart_ref, csrc_ref, owner_ref,
    tod, mask, model, res_hi, res_lo,
    part, acc, got_c, got_p, acc2, got3, amp,
    lhs_p, lhs_m, band,
    slots, dets, first_tile, shift, tod_snip, good_snip, snip, cnt, cnt_got, tsum, tsum_got,
    in_sem, small_sem, ready_sem, c_sem, p_sem, r_sem, g_sem, gc_sem, t_sem,
):
    wafer = lax.axis_index("wafer")
    det = lax.axis_index("det")
    core = lax.rem(det, 2)
    x = lax.rem(lax.div(det, 2), RING)
    y = lax.div(det, 2 * RING)
    coord = {"x": x, "y": y, "z": wafer}

    def reach(steps):
        at = {a: lax.rem(coord[a] + steps[a], RING) if steps.get(a) else coord[a] for a in coord}
        return (at["z"], (at["y"] * RING + at["x"]) * 2 + core)

    partner = (wafer, det + 1 - 2 * core)

    def remote(src, dst, send, recv, to):
        return pltpu.make_async_remote_copy(
            src_ref=src, dst_ref=dst, send_sem=send, recv_sem=recv,
            device_id=to, device_id_type=MESH,
        )

    def cols(first, width):
        return pl.ds(pl.multiple_of(first, 128), width)

    small = []
    for k, (src, dst) in enumerate((
        (coup_hbm, coup_ref), (taps_hbm, taps_ref), (cdet_hbm, cdet_ref),
        (cstart_hbm, cstart_ref), (csrc_hbm, csrc_ref), (owner_hbm, owner_ref),
    )):
        small.append(pltpu.make_async_copy(src, dst, small_sem.at[k]))
        small[-1].start()

    halves = (1 - core, core)
    loads = {}
    for g in range(len(GROUPS)):
        for h in range(2):
            span = cols(halves[h] * HALF + g * WIDE, WIDE)
            loads[h, g] = (
                pltpu.make_async_copy(tod_hbm.at[:, span], tod.at[:, span], in_sem.at[h, g, 0]),
                pltpu.make_async_copy(mask_hbm.at[:, span], mask.at[:, span], in_sem.at[h, g, 1]),
            )
            for one in loads[h, g]:
                one.start()

    lines = [reach({a: step}) for a in ("x", "y", "z") for step in range(1, RING)]
    barrier = pltpu.get_barrier_semaphore()
    for to in [partner] + lines:
        pl.semaphore_signal(barrier, inc=1, device_id=to, device_id_type=MESH)

    small[0].wait()
    coup_t = coup_ref[...]
    t_hi, t_lo = split(coup_t)
    w_hi, w_lo = split(coup_t * coup_t)
    zero = jnp.zeros((MODES, ROWS), BF16)
    lhs_p[0:32, :] = jnp.concatenate([t_hi, t_lo, t_hi, zero], axis=1)
    lhs_p[32:64, :] = jnp.concatenate([zero, zero, zero, w_hi], axis=1)
    lhs_p[64:96, :] = jnp.concatenate([zero, zero, zero, w_lo], axis=1)

    def partial_sums(first, width):
        span = cols(first, width)
        m = mask[:, span]
        v = jnp.where(m != 0, tod[:, span], 0.0)
        v_hi, v_lo = split(v)
        g = m.astype(F32).astype(BF16)
        out = dot(lhs_p[...], jnp.concatenate([v_hi, v_hi, v_lo, g], axis=0))
        return out[0:32], out[32:64] + out[64:96]

    def fill(h, g, dst):
        for one in loads[h, g]:
            one.wait()

        def body(i, carry):
            local = g * WIDE + i * CHUNK
            sums, weights = partial_sums(halves[h] * HALF + local, CHUNK)
            span = cols(local, CHUNK)
            for j in range(RING):
                dst[j, 0:8, span] = sums[8 * j:8 * j + 8]
                dst[j, 8:16, span] = weights[8 * j:8 * j + 8]
            return carry

        lax.fori_loop(0, WIDE // CHUNK, body, 0, unroll=True)

    copies_c = []
    for g in range(len(GROUPS)):
        span = pl.ds(g * WIDE, WIDE)
        copies_c.append(
            remote(part.at[:, :, span], got_c.at[:, :, span], c_sem.at[g, 0], c_sem.at[g, 1], partner)
        )
    fill(0, 0, part)
    pl.semaphore_wait(barrier, 1 + len(lines))
    copies_c[0].start()
    for to in lines:
        pl.semaphore_signal(ready_sem, inc=1, device_id=to, device_id_type=MESH)
    fill(1, 0, acc)
    fill(0, 1, part)
    copies_c[1].start()

    steps = sorted(
        ((p, q) for p in range(RING) for q in range(RING) if p or q),
        key=lambda v: -(min(v[0], RING - v[0]) + min(v[1], RING - v[1])),
    )
    on_line = [v for v in steps if not (v[0] and v[1])]
    off_line = [v for v in steps if v[0] and v[1]]

    def scatter(s, which):
        base, width, order = SETS[s]
        for p, q in which:
            block = cols(base + lax.rem(coord[order[0]] + p, RING) * width, width)
            remote(
                acc.at[lax.rem(coord[order[1]] + q, RING), :, block],
                got_p.at[steps.index((p, q)), :, pl.ds(PLACE[s], width)],
                p_sem.at[s, 0], p_sem.at[s, 1], reach({order[0]: p, order[1]: q}),
            ).start()

    def take(g):
        copies_c[g].wait_recv()
        span = pl.ds(g * WIDE, WIDE)
        acc[:, :, span] += got_c[:, :, span]

    take(0)
    for v in on_line:
        for s in GROUPS[0]:
            scatter(s, [v])
    fill(1, 1, acc)
    pl.semaphore_wait(ready_sem, len(lines))
    for v in off_line:
        for s in GROUPS[0]:
            scatter(s, [v])
    take(1)
    for v in steps:
        for s in GROUPS[1]:
            scatter(s, [v])

    for one in small[2:]:
        one.wait()
    owner = 2 * owner_ref[...]
    src_iota = lax.broadcasted_iota(jnp.int32, (128, CROSS), 0)
    of_src = (src_iota == csrc_ref[...]).astype(F32).astype(BF16)
    row_iota = lax.broadcasted_iota(jnp.int32, (256, 128), 0)
    perm0 = (row_iota == owner).astype(F32).astype(BF16)
    perm1 = (row_iota == owner + 1).astype(F32).astype(BF16)
    oh_t = jnp.concatenate([dot(perm0, of_src), dot(perm1, of_src)], axis=1)
    slots[:, 0:128] = oh_t.astype(BF16)
    slots[:, 128:256] = oh_t.astype(BF16)
    det_iota = lax.broadcasted_iota(jnp.int32, (ROWS, CROSS), 0)
    of_det = (det_iota == cdet_ref[...]).astype(F32).T.astype(BF16)
    dets[...] = jnp.concatenate([of_det, of_det], axis=1)
    start = jnp.broadcast_to(cstart_ref[...], (128, CROSS)).T
    first_tile[...] = start >> 7
    shift[...] = start & 127
    c_hi, c_lo = split(coup_ref[...].T)
    lhs_m[0:ROWS, :] = jnp.concatenate([c_hi, c_lo, c_hi], axis=1)
    lhs_m[ROWS:ROWS + CROSS, :] = dot(of_det, lhs_m[0:ROWS, :]).astype(BF16)
    cnt[...] = jnp.broadcast_to(jnp.sum(oh_t, axis=1, keepdims=True), (256, 128)).reshape(DET, 8, 128)

    small[1].wait()
    line = jnp.concatenate([taps_ref[...], jnp.zeros((1, 256 - TAPS), F32)], axis=1)
    turned = pltpu.roll(jnp.broadcast_to(line, (128, 256)), 192, 1, stride=1, stride_axis=0)
    b_hi, b_lo = split(turned.T)
    band[:, 0:128] = b_hi
    band[:, 128:256] = b_lo

    def choose(b, lines, wide):
        tile = first_tile[...]
        at = {v: tile == b * 4 + v for v in range(-2, 4)}
        wide = list(wide)
        for q in range(4):
            for w in range(3):
                for k, line in enumerate(lines):
                    wide[3 * k + w] = jnp.where(at[q - w], line[:, 128 * q:128 * q + 128], wide[3 * k + w])
        return tuple(wide)

    def shifted(wide):
        rows = jnp.concatenate(wide, axis=1)
        rest = jnp.concatenate([shift[...]] * 3, axis=1)
        for bit in range(7):
            moved = pltpu.roll(rows, 384 - (1 << bit), 1)
            rows = jnp.where((rest & (1 << bit)) != 0, moved, rows)
        return rows[:, 0:256]

    no_tiles = (jnp.zeros((CROSS, 128), F32),) * 3

    def input_block(b, wide):
        span = cols(b * 512, 512)
        m = mask[:, span]
        v_hi, v_lo = split(jnp.where(m != 0, tod[:, span], 0.0))
        g = m.astype(F32).astype(BF16)
        lines = dot(dets[...], jnp.concatenate([v_hi, v_lo], axis=0)), dot(dets[:, 0:ROWS], g)
        return choose(b, lines, wide)

    inputs = lax.fori_loop(0, NS // 512, input_block, no_tiles * 2)
    tod_snip[...] = shifted(inputs[0:3])
    good_snip[...] = shifted(inputs[3:6])
    for edge in (res_hi, res_lo):
        edge[:, 0:128] = jnp.zeros((ROWS, 128), BF16)
        edge[:, 128 + NS:256 + NS] = jnp.zeros((ROWS, 128), BF16)

    def from_plane(s, rows, sems):
        every = got_p.at[:, 0:rows, pl.ds(PLACE[s], SETS[s][1])]
        return remote(every, every, sems.at[s, 0], sems.at[s, 1], partner)

    axis3 = []
    for s, (base, width, order) in enumerate(SETS):
        from_plane(s, 16, p_sem).wait_recv()
        span = pl.ds(PLACE[s], width)
        total = acc[coord[order[1]], :, cols(base + coord[order[0]] * width, width)]
        for k in range(len(steps)):
            total += got_p[k, :, span]
        acc2[:, span] = total
        for step in range(1, RING):
            axis3.append(remote(
                acc2.at[:, span], got3.at[step - 1, :, span],
                r_sem.at[s, step - 1, 0], r_sem.at[s, step - 1, 1], reach({order[2]: step}),
            ))
            axis3[-1].start()

    for members in GROUPS:
        here = {}
        for s in members:
            base, width, order = SETS[s]
            for one in axis3[3 * s:3 * s + 3]:
                one.wait_recv()
            span = pl.ds(PLACE[s], width)
            whole = (acc2[:, span] + got3[0, :, span]) + (got3[1, :, span] + got3[2, :, span])
            block = cols(core * HALF + base + coord[order[0]] * width, width)
            amp[coord[order[1]], :, block] = whole[0:8] / (whole[8:16] + 1.0)
            here[s] = amp.at[coord[order[1]], :, block]
        for p, q in steps:
            for s in members:
                to = reach({SETS[s][2][0]: p, SETS[s][2][1]: q})
                remote(here[s], here[s], g_sem.at[s, 0], g_sem.at[s, 1], to).start()

    owners = []
    for p, q in steps + [(0, 0)]:
        for other in (0, 1):
            if p or q or other:
                at = reach({"x": p, "y": q})[1]
                owners.append(at + other * (1 - 2 * core))

    def to_owners(src, dst, send, recv):
        for k, to in enumerate(owners):
            remote(src.at[to], dst.at[k], send, recv, (wafer, to)).start()

    def model_block(b, wide):
        span = cols(b * 512, 512)
        a_hi, a_lo = split(amp[:, :, span].reshape(MODES, 512))
        value = dot(lhs_m[...], jnp.concatenate([a_hi, a_hi, a_lo], axis=0))
        model[:, span] = value[0:ROWS]
        return choose(b, (value[ROWS:ROWS + CROSS],), wide)

    def resid_blocks(side, g):
        for b in range(WIDE // CHUNK):
            first = side * HALF + g * WIDE + b * CHUNK
            span = cols(first, CHUNK)
            r_hi, r_lo = split(jnp.where(mask[:, span] != 0, tod[:, span] - model[:, span], 0.0))
            res_hi[:, cols(first + 128, CHUNK)] = r_hi
            res_lo[:, cols(first + 128, CHUNK)] = r_lo

    def model_blocks(side, g, wide):
        for b in range(WIDE // CHUNK):
            wide = model_block((side * HALF + g * WIDE) // CHUNK + b, wide)
        return wide

    wide = no_tiles
    copies_a = []
    for g, members in enumerate(GROUPS):
        for s in members:
            from_plane(s, 8, g_sem).wait_recv()
        half = amp.at[:, :, cols(core * HALF + g * WIDE, WIDE)]
        copies_a.append(remote(half, half, gc_sem.at[g, 0], gc_sem.at[g, 1], partner))
        copies_a[g].start()
        wide = model_blocks(core, g, wide)
        if g == 0:
            to_owners(cnt, cnt_got, t_sem.at[0], t_sem.at[1])
        resid_blocks(core, g)
        if g > 0:
            resid_blocks(1 - core, g - 1)
        copies_a[g].wait_recv()
        wide = model_blocks(1 - core, g, wide)

    rows = jnp.where(good_snip[...] != 0.0, tod_snip[...] - shifted(wide), 0.0)
    snip[0:CROSS, :] = rows[:, 0:128]
    snip[CROSS:2 * CROSS, :] = rows[:, 128:256]
    s_hi, s_lo = split(snip[...])
    tsum[...] = dot(slots[...], jnp.concatenate([s_hi, s_lo], axis=0)).reshape(DET, 8, 128)
    to_owners(tsum, tsum_got, t_sem.at[2], t_sem.at[3])

    resid_blocks(1 - core, len(GROUPS) - 1)
    lane64 = lax.broadcasted_iota(jnp.int32, (ROWS, 128), 1) < 64

    def fill_block(b, carry):
        pieces = []
        for res in (res_hi, res_lo):
            left = []
            for q in range(4):
                before = res[:, cols(b * 512 + q * 128, 128)]
                here = res[:, cols(b * 512 + q * 128 + 128, 128)]
                after = res[:, cols(b * 512 + q * 128 + 256, 128)]
                left.append(jnp.concatenate([here, jnp.where(lane64, after, before)], axis=1))
            pieces.append(jnp.concatenate(left, axis=0))
        l_hi, l_lo = pieces
        first = dot(l_hi, band[...])
        second = dot(l_lo, band[:, 0:128])
        smooth = first[:, 0:128] + (first[:, 128:256] + second)
        for q in range(4):
            span = cols(b * 512 + q * 128, 128)
            filled[:, span] = jnp.where(
                mask[:, span] != 0, tod[:, span], model[:, span] + smooth[q * ROWS:(q + 1) * ROWS]
            )
        return carry

    lax.fori_loop(0, NS // 512, fill_block, 0)

    def wait_all(src, dst, send, recv):
        every = remote(src.at[0:DET - 1], dst.at[0:DET - 1], send, recv, partner)
        every.wait_recv()
        every.wait_send()

    for one in copies_c + copies_a + axis3:
        one.wait_send()
    for s in range(len(SETS)):
        from_plane(s, 16, p_sem).wait_send()
        from_plane(s, 8, g_sem).wait_send()

    wait_all(cnt, cnt_got, t_sem.at[0], t_sem.at[1])
    number = cnt[det]
    for k in range(DET - 1):
        number += cnt_got[k]
    wait_all(tsum, tsum_got, t_sem.at[2], t_sem.at[3])
    total = tsum[det]
    for k in range(DET - 1):
        total += tsum_got[k]
    snip[0:8, :] = total / (number + 1.0)
    for o in range(4):
        templ_ref[0, o:o + 1, 0:128] = snip[2 * o:2 * o + 1, :]
        templ_ref[0, o:o + 1, 128:256] = snip[2 * o + 1:2 * o + 2, :]


def hand_out(filled, templ, filled_out, templ_out, sem):
    copies = [pltpu.make_async_copy(templ, templ_out, sem.at[8])]
    for k in range(8):
        strip = pl.ds(8 * k, 8)
        copies.append(pltpu.make_async_copy(filled.at[strip], filled_out.at[strip], sem.at[k]))
    for one in copies:
        one.start()
    for one in copies:
        one.wait()


def on_device(tod, gap_mask, coupling, taps, cross_det, cross_start, cross_src, src_owner):
    vmem, hbm = (pl.BlockSpec(memory_space=m) for m in (pltpu.VMEM, pltpu.HBM))
    shapes = (jax.ShapeDtypeStruct((ROWS, NS), F32), jax.ShapeDtypeStruct((1, 4, 256), F32))
    results = pl.pallas_call(
        kernel,
        out_shape=shapes,
        in_specs=[hbm] * 8,
        out_specs=(vmem, vmem),
        scratch_shapes=[
            pltpu.VMEM((MODES, ROWS), F32),
            pltpu.VMEM((1, TAPS), F32),
            pltpu.VMEM((1, CROSS), jnp.int32),
            pltpu.VMEM((1, CROSS), jnp.int32),
            pltpu.VMEM((1, CROSS), jnp.int32),
            pltpu.VMEM((1, 128), jnp.int32),
            pltpu.VMEM((ROWS, NS), F32),
            pltpu.VMEM((ROWS, NS), jnp.int32),
            pltpu.VMEM((ROWS, NS), F32),
            pltpu.VMEM((ROWS, NS + 256), BF16),
            pltpu.VMEM((ROWS, NS + 256), BF16),
            pltpu.VMEM((RING, 16, HALF), F32),
            pltpu.VMEM((RING, 16, HALF), F32),
            pltpu.VMEM((RING, 16, HALF), F32),
            pltpu.VMEM((RING * RING - 1, 16, BLOCKS), F32),
            pltpu.VMEM((16, BLOCKS), F32),
            pltpu.VMEM((3, 16, BLOCKS), F32),
            pltpu.VMEM((RING, 8, NS), F32),
            pltpu.VMEM((96, 256), BF16),
            pltpu.VMEM((ROWS + CROSS, 96), BF16),
            pltpu.VMEM((256, 256), BF16),
            pltpu.VMEM((256, 256), BF16),
            pltpu.VMEM((CROSS, 128), BF16),
            pltpu.VMEM((CROSS, 128), jnp.int32),
            pltpu.VMEM((CROSS, 128), jnp.int32),
            pltpu.VMEM((CROSS, 256), F32),
            pltpu.VMEM((CROSS, 256), F32),
            pltpu.VMEM((2 * CROSS, 128), F32),
            pltpu.VMEM((DET, 8, 128), F32),
            pltpu.VMEM((DET, 8, 128), F32),
            pltpu.VMEM((DET, 8, 128), F32),
            pltpu.VMEM((DET, 8, 128), F32),
            pltpu.SemaphoreType.DMA((2, 2, 2)),
            pltpu.SemaphoreType.DMA((6,)),
            pltpu.SemaphoreType.REGULAR,
            pltpu.SemaphoreType.DMA((2, 2)),
            pltpu.SemaphoreType.DMA((6, 2)),
            pltpu.SemaphoreType.DMA((6, 3, 2)),
            pltpu.SemaphoreType.DMA((6, 2)),
            pltpu.SemaphoreType.DMA((2, 2)),
            pltpu.SemaphoreType.DMA((4,)),
        ],
        compiler_params=pltpu.CompilerParams(
            collective_id=0, has_side_effects=True, vmem_limit_bytes=40 << 20
        ),
    )(*(pltpu.with_memory_space_constraint(v, pltpu.HBM) for v in (tod, gap_mask, coupling.T, *(v.reshape(1, -1) for v in (taps, cross_det, cross_start, cross_src, src_owner)))))

    return pl.pallas_call(
        hand_out,
        out_shape=shapes,
        in_specs=[vmem] * 2,
        out_specs=(hbm, hbm),
        scratch_shapes=[pltpu.SemaphoreType.DMA((9,))],
        compiler_params=pltpu.CompilerParams(vmem_limit_bytes=1 << 20),
    )(*results)


def solution(mesh):
    return jax.shard_map(
        on_device,
        mesh=mesh,
        in_specs=(
            P(("wafer", "det"), None),
            P(("wafer", "det"), None),
            P(("wafer", "det"), None),
            P(),
            P(("wafer", "det")),
            P(("wafer", "det")),
            P(("wafer", "det")),
            P(),
        ),
        out_specs=(P(("wafer", "det"), None), P("wafer", "det", None)),
        check_vma=False,
    )
```
